128 devices in a mesh: dp: 4 (over z), seq: 32 (over x, y, core).
Axes of the slice: x: 4, y: 4, z: 4, core: 2. Of those that a mesh axis runs over, the one named last changes fastest.
Arguments:
- mixed: bfloat16 [4, 4096, 4096], P('dp', 'seq'), may hold values from -6 to 6
- conv_weight: bfloat16 [4, 4096], replicated, may hold values from -3 to 3
- log_decay: float32 [4, 16, 4096], P('dp', None, 'seq'), may hold values from -0.75 to 0, as said below
- beta: float32 [4, 16, 4096], P('dp', None, 'seq'), may hold values from 0.01 to 0.5
- doc_ids: int32 [4, 4096], P('dp', 'seq'), may hold values from 0 to 7, never falling along the last dimension, each value on 1 to 1024 neighbouring positions
- out_grad: bfloat16 [4, 4096, 2048], P('dp', 'seq'), may hold values from -6 to 6
Outputs:
- output: bfloat16 [4, 4096, 2048], P('dp', 'seq')
- d_mixed: bfloat16 [4, 4096, 4096], P('dp', 'seq')
- d_conv_weight: float32 [4, 4096], replicated
- d_log_decay: float32 [4, 16, 4096], P('dp', None, 'seq')
- d_beta: float32 [4, 16, 4096], P('dp', None, 'seq')
The draws below stay inside these ranges and needn't reach their ends.
Inputs may be any that keep to these rules, and one draw needn't show every extreme that they name: `doc_ids`: document numbers never fall along a slab; each of the 8 documents holds 1 to 1024 tokens, and one holds exactly 1024. `log_decay`: every entry is negative.
All inputs are finite; a program needn't handle non-finite values.
Results may differ from the reference program's by a relative error of at most 0.00115.
Values may be sent and summed in bfloat16 or wider, within the bound.
A program may use at most 128 MiB of HBM per device.

```python
import math
import jax
import jax.numpy as jnp
import numpy as np
from jax import lax

DK = 128
KH = 8
VH = 16
CH = 64
DOCS = 8
C = 4096
SLABS = 4
PIECE_LENGTH = 4096
DOC_MOST = 1024


def draw_log_decay(key, part):
    document_streams = jax.random.split(key, 4)
    lowest = math.log(0.25 / PIECE_LENGTH)
    upper = math.log(1.0 / 30.0)
    tensor_extent = (SLABS, VH, PIECE_LENGTH)
    gating_numbers = jnp.exp(jax.random.uniform(document_streams[0], (SLABS, VH, 1), jnp.float32, lowest, upper))
    approximate_guess = jax.random.uniform(document_streams[1], tensor_extent, jnp.float32, 0.5, 1.5)
    packet_clusters = (jax.random.uniform(document_streams[2], tensor_extent, jnp.float32) < 3.0 / PIECE_LENGTH).astype(jnp.float32)
    nesting_level = jax.random.uniform(document_streams[3], tensor_extent, jnp.float32, 0.22, 0.69)
    return -(gating_numbers * approximate_guess) - packet_clusters * nesting_level


def level_of(own_key, dims, cuts, smallest, top_value):
    factor_of, own = 1.0, jax.random.fold_in(own_key, 6)
    for dim, parts in cuts:
        steps = jnp.exp(jax.random.uniform(jax.random.fold_in(own, dim), (parts,), jnp.float32, smallest / len(cuts), top_value / len(cuts)))
        factor_of = factor_of * jnp.repeat(steps, dims[dim] // parts).reshape([-1 if axis == dim else 1 for axis in range(len(dims))])
    return factor_of


def profile(count, total, most, slope):
    loads = [(1 << 20) // math.isqrt(rank ** slope) + 1 for rank in range(2, count + 1)]
    surplus, holding = total - most - (count - 1), [1] * (count - 1)
    while surplus > 0:
        movable = [i for i in range(count - 1) if holding[i] < most]
        pool, remaining = sum([loads[i] for i in movable]), surplus
        for i in movable:
            more = min(most - holding[i], max(1, remaining * loads[i] // pool), surplus)
            holding[i] = holding[i] + more
            surplus = surplus - more
    return np.array([most] + holding)


def ragged(key, count, total, most, lean):
    if count == 2:
        one = jax.random.randint(key, (), max(1, total - most), min(most, total - 1) + 1)
        return jnp.stack([one, total - one])
    tallies = jnp.asarray(profile(count, total, most, lean), jnp.int32)
    twos = (count - 1) // 2
    giver, sink = tallies[1:1 + 2 * twos:2], tallies[2:2 + 2 * twos:2]
    slack = jnp.minimum(giver - 1, most - sink)
    shifted = jax.random.randint(jax.random.fold_in(key, 1), (twos,), 0, 1 << 20) % (slack + 1)
    tallies = tallies.at[1:1 + 2 * twos:2].set(giver - shifted).at[2:2 + 2 * twos:2].set(sink + shifted)
    return tallies[jax.random.permutation(jax.random.fold_in(key, 2), count)]


def gaussian(stream_key, shape, width, most, cuts=(), held_as=jnp.bfloat16):
    gain = level_of(stream_key, shape, cuts, -0.22, 0.18) if cuts else 1.0
    result = jax.random.normal(stream_key, shape, jnp.float32) * width * gain
    return jnp.minimum(jnp.maximum(result, -most), most).astype(held_as)


def setup_inputs(seed: int = 0) -> dict:
    streams_of = jax.random.split(jax.random.key(seed), 7)
    mixed = gaussian(streams_of[0], (SLABS, PIECE_LENGTH, C), 1.0, 6.0, ((0, 4), (1, 32)))
    conv_weight = gaussian(streams_of[1], (4, C), 4 ** -0.5, 3.0)
    log_decay = draw_log_decay(jax.random.fold_in(streams_of[6], 71), 0)
    beta = jnp.clip(jnp.exp(math.log(0.5) - 3.912023 * jax.random.uniform(streams_of[3], (SLABS, VH, PIECE_LENGTH), jnp.float32) ** level_of(streams_of[3], (SLABS, VH, PIECE_LENGTH), ((0, 4), (2, 32)), -0.2, 0.2)), 0.01, 0.5)
    doc_ids = jax.vmap(lambda own: jnp.searchsorted(jnp.cumsum(ragged(own, DOCS, PIECE_LENGTH, DOC_MOST, 2)), jnp.arange(PIECE_LENGTH), side="right"))(jax.random.split(streams_of[4], SLABS)).reshape((SLABS, PIECE_LENGTH)).astype(jnp.int32)
    out_grad = gaussian(streams_of[5], (SLABS, PIECE_LENGTH, VH * DK), 1.0, 6.0, ((0, 4), (1, 32)))
    return dict(mixed=mixed, conv_weight=conv_weight, log_decay=log_decay, beta=beta, doc_ids=doc_ids, out_grad=out_grad)


highest_precision = lax.Precision.HIGHEST
epsilon = 1e-06

def unit_norm(values):
    return values * lax.rsqrt(lax.optimization_barrier(jnp.sum(values * values, -1, keepdims=True)) + epsilon)

def conv_active(rows, weight, documents):
    summed = weight[3] * rows
    for offset in (1, 2, 3):
        moved = jnp.concatenate([jnp.zeros((offset, rows.shape[1]), jnp.float32), rows[:-offset]], 0)
        moved_docs = jnp.concatenate([jnp.full((offset,), -1, jnp.int32), documents[:-offset]], 0)
        summed = summed + weight[3 - offset] * jnp.where((moved_docs == documents)[:, None], moved, 0.0)
    return jax.nn.silu(summed)

def token_step(memory_state, item):
    query_matrix, key_rows, values, fading, rate, starting = item
    memory_state = jnp.where(starting, 0.0, memory_state)
    project_input = jnp.einsum('es,esz->ez', key_rows, memory_state, precision=highest_precision)
    memory_state = fading[:, None, None] * (memory_state - rate[:, None, None] * key_rows[:, :, None] * project_input[:, None, :])
    memory_state = memory_state + rate[:, None, None] * key_rows[:, :, None] * values[:, None, :]
    emitted_output = jnp.einsum('es,esz->ez', query_matrix, memory_state, precision=highest_precision)
    return (memory_state, emitted_output)

@jax.checkpoint
def block_step(memory_state, item):
    return lax.scan(token_step, memory_state, item)

def forward(rows, weight, decay, rate, documents):
    length = rows.shape[0]
    active = conv_active(rows, weight, documents)
    query_matrix = active[:, :KH * DK].reshape(length, KH, DK)
    key_rows = active[:, KH * DK:2 * KH * DK].reshape(length, KH, DK)
    values = active[:, 2 * KH * DK:].reshape(length, VH, DK)
    query_matrix = jnp.repeat(unit_norm(query_matrix) * DK ** (-0.5), VH // KH, axis=1)
    key_rows = jnp.repeat(unit_norm(key_rows), VH // KH, axis=1)
    fading = jnp.exp(decay.T)
    starting = documents != jnp.concatenate([jnp.full((1,), -1, jnp.int32), documents[:-1]], 0)
    blocks = length // CH
    items = (query_matrix.reshape(blocks, CH, VH, DK), key_rows.reshape(blocks, CH, VH, DK), values.reshape(blocks, CH, VH, DK), fading.reshape(blocks, CH, VH), rate.T.reshape(blocks, CH, VH), starting.reshape(blocks, CH))
    initial = jnp.zeros((VH, DK, DK), jnp.float32)
    final_state, emitted_output = lax.scan(block_step, initial, items)
    return emitted_output.reshape(length, VH * DK)

def reference(mixed, conv_weight, log_decay, beta, doc_ids, out_grad):
    weight = conv_weight.astype(jnp.float32)

    def one_slab(item):
        rows, decay, rate, documents, cotangent = item

        def local_forward(rows_in, weight_in, decay_in, rate_in):
            return forward(rows_in, weight_in, decay_in, rate_in, documents)
        read, pullback = jax.vjp(local_forward, rows.astype(jnp.float32), weight, decay, rate)
        grad_rows, grad_weight, grad_decay, grad_rate = pullback(cotangent.astype(jnp.float32))
        return (read.astype(jnp.bfloat16), grad_rows.astype(jnp.bfloat16), grad_weight, grad_decay, grad_rate)
    results = lax.map(one_slab, (mixed, log_decay, beta, doc_ids, out_grad))
    return (results[0], results[1], lax.optimization_barrier(jnp.sum(results[2], 0)), results[3], results[4])
```

```python
import functools

import jax
import jax.numpy as jnp
from jax import lax
from jax.experimental import pallas as pl
from jax.experimental.pallas import tpu as pltpu
from jax.sharding import PartitionSpec as P

DK = 128
KH = 8
VH = 16
L = 128
GROUP = 8
QUARTER = GROUP * 128
NB = QUARTER // L
PER = 2
EPS = 1e-6

f32 = jnp.float32
bf16 = jnp.bfloat16
NN = (((1,), (0,)), ((), ()))
NT = (((1,), (1,)), ((), ()))
MESH = pl.DeviceIdType.MESH
VM = pltpu.VMEM
vspec = pl.BlockSpec(memory_space=pltpu.VMEM)
sspec = pl.BlockSpec(memory_space=pltpu.SMEM)


def split(a):
    high = a.astype(bf16)
    return high, (a - high.astype(f32)).astype(bf16)


def one(a):
    return (a.astype(bf16),)


def mm(a, b, dims=NN):
    def dot(p, q):
        return lax.dot_general(p, q, dims, preferred_element_type=f32)

    total = dot(a[0], b[0])
    if len(b) > 1:
        total = total + dot(a[0], b[1])
    if len(a) > 1:
        total = total + dot(a[1], b[0])
    return total


def exact(a, b):
    return lax.dot_general(a, b, NN, preferred_element_type=f32, precision=lax.Precision.HIGHEST)


def iotas():
    return (
        lax.broadcasted_iota(jnp.int32, (L, L), 0),
        lax.broadcasted_iota(jnp.int32, (L, L), 1),
    )


def heads_kernel(
    mixed, grad, aux, out_mixed, out_grad, out_aux, halo_mixed, halo_aux, send, recv, hsend, hrecv
):
    dp = lax.axis_index("dp")
    me = lax.axis_index("seq")
    row, j = me // GROUP, lax.rem(me, GROUP)
    base = row * GROUP
    last = GROUP - 1
    before = lax.rem(row + 3, 4) * GROUP
    after = lax.rem(row + 1, 4) * GROUP
    is_last = j == last

    barrier = pltpu.get_barrier_semaphore()
    for s in range(1, GROUP):
        pl.semaphore_signal(
            barrier, inc=1, device_id=(dp, base + lax.rem(j + s, GROUP)), device_id_type=MESH
        )
    pl.semaphore_signal(barrier, inc=1, device_id=(dp, before + last), device_id_type=MESH)
    pl.semaphore_wait(barrier, jnp.where(is_last, 2 * GROUP - 1, GROUP - 1))

    def pieces(to, start, rows):
        q = pl.ds(pl.multiple_of(to * DK, DK), DK)
        k = pl.ds(pl.multiple_of((KH + to) * DK, DK), DK)
        v = pl.ds(pl.multiple_of((2 * KH + 2 * to) * DK, 2 * DK), 2 * DK)
        r = pl.ds(start, rows)
        return mixed.at[r, q], mixed.at[r, k], mixed.at[r, v]

    copies = []
    place = pl.ds(pl.multiple_of(j * 128, 128), 128)
    for s in range(1, GROUP):
        to = lax.rem(j + s, GROUP)
        q, k, v = pieces(to, 0, 128)
        g = grad.at[:, pl.ds(pl.multiple_of(to * 2 * DK, 2 * DK), 2 * DK)]
        pairs = (
            (q, out_mixed.at[place, pl.ds(0, DK)]),
            (k, out_mixed.at[place, pl.ds(DK, DK)]),
            (v, out_mixed.at[place, pl.ds(2 * DK, 2 * DK)]),
            (aux.at[to], out_aux.at[j]),
            (g, out_grad.at[place, :]),
        )
        for i, (src, dst) in enumerate(pairs):
            copy = pltpu.make_async_remote_copy(
                src_ref=src,
                dst_ref=dst,
                send_sem=send.at[s, i],
                recv_sem=recv.at[s, i],
                device_id=(dp, base + to),
                device_id_type=MESH,
            )
            copy.start()
            copies.append(copy)

    def halo_copies(to):
        q, k, v = pieces(to, 112, 16)
        pairs = (
            (q, halo_mixed.at[:, pl.ds(0, DK)]),
            (k, halo_mixed.at[:, pl.ds(DK, DK)]),
            (v, halo_mixed.at[:, pl.ds(2 * DK, 2 * DK)]),
            (aux.at[to], halo_aux.at[:, :]),
        )
        return [
            pltpu.make_async_remote_copy(
                src_ref=src,
                dst_ref=dst,
                send_sem=hsend.at[to, i],
                recv_sem=hrecv.at[i],
                device_id=(dp, after + to),
                device_id_type=MESH,
            )
            for i, (src, dst) in enumerate(pairs)
        ]

    @pl.when(is_last)
    def _():
        for to in range(GROUP):
            for copy in halo_copies(to):
                copy.start()

    out_mixed[place, 0:DK] = mixed[:, pl.ds(pl.multiple_of(j * DK, DK), DK)]
    out_mixed[place, DK : 2 * DK] = mixed[:, pl.ds(pl.multiple_of((KH + j) * DK, DK), DK)]
    out_mixed[place, 2 * DK :] = mixed[
        :, pl.ds(pl.multiple_of((2 * KH + 2 * j) * DK, 2 * DK), 2 * DK)
    ]
    out_grad[place, :] = grad[:, pl.ds(pl.multiple_of(j * 2 * DK, 2 * DK), 2 * DK)]
    out_aux[j] = aux[j]

    for copy in copies:
        copy.wait()
    for copy in halo_copies(0):
        copy.wait_recv()

    @pl.when(is_last)
    def _():
        for to in range(GROUP):
            for copy in halo_copies(to):
                copy.wait_send()


def to_heads(mixed, grad, aux):
    return pl.pallas_call(
        heads_kernel,
        out_shape=(
            jax.ShapeDtypeStruct((QUARTER, 4 * DK), bf16),
            jax.ShapeDtypeStruct((QUARTER, 2 * DK), bf16),
            jax.ShapeDtypeStruct((GROUP, 8, 128), f32),
            jax.ShapeDtypeStruct((16, 4 * DK), bf16),
            jax.ShapeDtypeStruct((8, 128), f32),
        ),
        in_specs=[vspec] * 3,
        out_specs=(vspec,) * 5,
        scratch_shapes=[
            pltpu.SemaphoreType.DMA((GROUP, 5)),
            pltpu.SemaphoreType.DMA((GROUP, 5)),
            pltpu.SemaphoreType.DMA((GROUP, 4)),
            pltpu.SemaphoreType.DMA((4,)),
        ],
        compiler_params=pltpu.CompilerParams(collective_id=0, has_side_effects=True),
        name="to_heads",
    )(mixed, grad, aux)


def gates(tile, h, doc_column, doc_row, doc_before, columns):
    ri, ci = iotas()
    cum = columns[:, h : h + 1]
    cum_row = tile[h : h + 1, :]
    rate = columns[:, 2 + h : 3 + h]
    cum_last = tile[h : h + 1, L - 1 : L]
    doc_last = tile[4:5, L - 1 : L]
    same = doc_column == doc_row
    fade = jnp.where(same & (ri >= ci), jnp.exp(jnp.minimum(cum - cum_row, 0.0)), 0.0)
    carry = doc_column == doc_before
    enter = jnp.where(carry, jnp.exp(cum), 0.0)
    tail = jnp.where(doc_column == doc_last, jnp.exp(cum_last - cum), 0.0)
    keep = jnp.where(doc_last == doc_before, jnp.exp(cum_last), 0.0)
    return fade, enter, tail, keep, rate


def first_kernel(
    meta, mixed, halo, grad, aux, halo_aux, weight, summed_o, q_o, k_o, tile_o, col_o, t_o, w_o, u_o,
    p_o, a_o, b_o, r_o, send_o, xs, ds,
):
    j, first = meta[0], meta[1]
    ri, ci = iotas()
    upper = jnp.where(ri <= ci, 1.0, 0.0).astype(f32)
    flat = aux[...].reshape(NB * 8, 128)
    sums = exact(flat, upper)
    which = lax.rem(lax.broadcasted_iota(jnp.int32, (NB * 8, 128), 0), 8)
    tile_o[...] = jnp.where(which < 2, sums, flat).reshape(NB, 8, 128)

    rows = PER * L
    halo_columns = jnp.transpose(halo_aux[...])
    halo_columns = jnp.where(first == 1, -1.0, halo_columns)
    xs[0:8, :] = halo[8:16, :].astype(f32)
    ds[0:8, :] = halo_columns[120:128, :]
    col_o[0:8, :] = halo_columns[120:128, :]

    wq = weight[:, pl.ds(pl.multiple_of(j * DK, DK), DK)].astype(f32)
    wk = weight[:, pl.ds(pl.multiple_of((KH + j) * DK, DK), DK)].astype(f32)
    wv = weight[:, pl.ds(pl.multiple_of((2 * KH + 2 * j) * DK, 2 * DK), 2 * DK)].astype(f32)
    taps = jnp.concatenate([wq, wk, wv], axis=1)

    def body(i, carry):
        r0 = pl.multiple_of(i * rows, rows)
        xs[8:, :] = mixed[pl.ds(r0, rows), :].astype(f32)
        tiles = [tile_o[i * PER + p] for p in range(PER)]
        for p in range(PER):
            ds[8 + p * L : 8 + (p + 1) * L, :] = jnp.transpose(tiles[p])
        col_o[pl.ds(pl.multiple_of(r0 + 8, 8), rows), :] = ds[8:, :]
        doc = ds[8:, 4:5]
        summed = taps[3:4, :] * xs[8:, :]
        for o in (1, 2, 3):
            same = ds[8 - o : 8 - o + rows, 4:5] == doc
            summed = summed + taps[3 - o : 4 - o, :] * jnp.where(
                same, xs[8 - o : 8 - o + rows, :], 0.0
            )
        summed_o[pl.ds(r0, rows), :] = summed
        active = summed / (1.0 + jnp.exp(-summed))
        q = active[:, :DK]
        k = active[:, DK : 2 * DK]
        q = q * lax.rsqrt(jnp.sum(q * q, -1, keepdims=True) + EPS) * DK**-0.5
        k = k * lax.rsqrt(jnp.sum(k * k, -1, keepdims=True) + EPS)
        q_o[pl.ds(r0, rows), :] = q
        k_o[pl.ds(r0, rows), :] = k

        chains = []
        for p in range(PER):
            lo = slice(p * L, (p + 1) * L)
            kp, qp = k[lo], q[lo]
            ks, qs = split(kp), split(qp)
            inner = mm(ks, ks, NT)
            score = mm(qs, ks, NT)
            doc_column = ds[8 + p * L : 8 + (p + 1) * L, 4:5]
            doc_row = tiles[p][4:5, :]
            doc_before = ds[7 + p * L : 8 + p * L, 4:5]
            columns = ds[8 + p * L : 8 + (p + 1) * L, :]
            for h in range(2):
                fade, enter, tail, keep, rate = gates(
                    tiles[p], h, doc_column, doc_row, doc_before, columns
                )
                low = jnp.where(ri > ci, rate * inner * fade, 0.0)
                vp = active[lo, (2 + h) * DK : (3 + h) * DK]
                chains.append(
                    dict(p=p, h=h, low=low, score=score * fade, enter=enter, tail=tail, keep=keep,
                         rate=rate, k=kp, q=qp, v=vp)
                )
        eye = jnp.where(ri == ci, 1.0, 0.0).astype(f32)
        size = 1
        inverse = None
        while size < L:
            mask = (ri // (2 * size) == ci // (2 * size)) & (
                lax.rem(ri // size, 2) == 1
            ) & (lax.rem(ci // size, 2) == 0)
            corners = [jnp.where(mask, c["low"], 0.0) for c in chains]
            if inverse is None:
                inverse = [eye - x for x in corners]
            else:
                parts = [split(x) for x in inverse]
                inner = [mm(split(c), x) for c, x in zip(corners, parts)]
                inverse = [
                    x - mm(y, split(z)) for x, y, z in zip(inverse, parts, inner)
                ]
            size *= 2
        for c, t in zip(chains, inverse):
            n = (i * PER + c["p"]) * 2 + c["h"]
            t_o[n] = t
            p_o[n] = c["score"]
            ts = split(t)
            w = mm(ts, split((c["rate"] * c["enter"]) * c["k"]))
            u = mm(ts, split(c["rate"] * c["v"]))
            w_o[n] = w
            u_o[n] = u
            kt = jnp.transpose(c["tail"] * c["k"])
            kts = split(kt)
            ws = split(w)
            a_o[n] = jnp.where(ri == ci, c["keep"], 0.0) - mm(kts, ws)
            b_o[n] = mm(split(jnp.transpose(u)), split(c["tail"] * c["k"]))
            g = grad[pl.ds(pl.multiple_of(r0 + c["p"] * L, L), L), c["h"] * DK : (c["h"] + 1) * DK]
            du = mm(split(jnp.transpose(c["score"])), (g,))
            gt = (jnp.transpose(g.astype(f32)).astype(bf16),)
            r_o[n] = mm(gt, split(c["enter"] * c["q"])) - mm(split(jnp.transpose(du)), ws)
        xs[0:8, :] = xs[rows : rows + 8, :]
        ds[0:8, :] = ds[rows : rows + 8, :]
        return carry

    lax.fori_loop(0, NB // PER, body, 0)

    def scan(i, carry):
        s0, s1, r0, r1 = carry
        m = NB - 1 - i
        out = []
        for h, s in ((0, s0), (1, s1)):
            out.append(mm(split(s), split(a_o[2 * i + h]), NT) + b_o[2 * i + h])
        for h, r in ((0, r0), (1, r1)):
            out.append(mm(split(r), split(a_o[2 * m + h])) + r_o[2 * m + h])
        return tuple(out)

    zero = jnp.zeros((DK, DK), f32)
    states = lax.fori_loop(0, NB, scan, (zero,) * 4)
    for i in range(4):
        send_o[i] = states[i]


def first_phase(meta, mixed, halo, grad, aux, halo_aux, weight, interpret=False):
    square = jax.ShapeDtypeStruct((2 * NB, DK, DK), f32)
    return pl.pallas_call(
        first_kernel,
        out_shape=(
            jax.ShapeDtypeStruct((QUARTER, 4 * DK), f32),
            jax.ShapeDtypeStruct((QUARTER, DK), f32),
            jax.ShapeDtypeStruct((QUARTER, DK), f32),
            jax.ShapeDtypeStruct((NB, 8, 128), f32),
            jax.ShapeDtypeStruct((8 + QUARTER, 8), f32),
        )
        + (square,) * 7
        + (jax.ShapeDtypeStruct((4, DK, DK), f32),),
        in_specs=[sspec] + [vspec] * 6,
        out_specs=(vspec,) * 13,
        scratch_shapes=[VM((8 + PER * L, 4 * DK), f32), VM((8 + PER * L, 8), f32)],
        compiler_params=pltpu.CompilerParams(vmem_limit_bytes=60 * 1024 * 1024),
        name="first_phase",
        interpret=interpret,
    )(meta, mixed, halo, grad, aux, halo_aux, weight)


def states_kernel(src, dst, send, recv):
    dp = lax.axis_index("dp")
    me = lax.axis_index("seq")
    after = lax.rem(me + GROUP, 4 * GROUP)
    before = lax.rem(me + 3 * GROUP, 4 * GROUP)
    barrier = pltpu.get_barrier_semaphore()
    for to in (after, before):
        pl.semaphore_signal(barrier, inc=1, device_id=(dp, to), device_id_type=MESH)
    pl.semaphore_wait(barrier, 2)
    copies = []
    for i, to in ((0, after), (1, before)):
        copy = pltpu.make_async_remote_copy(
            src_ref=src.at[pl.ds(2 * i, 2)],
            dst_ref=dst.at[pl.ds(2 * i, 2)],
            send_sem=send.at[i],
            recv_sem=recv.at[i],
            device_id=(dp, to),
            device_id_type=MESH,
        )
        copy.start()
        copies.append(copy)
    for copy in copies:
        copy.wait()


def exchange_states(states):
    return pl.pallas_call(
        states_kernel,
        out_shape=jax.ShapeDtypeStruct((4, DK, DK), f32),
        in_specs=[vspec],
        out_specs=vspec,
        scratch_shapes=[pltpu.SemaphoreType.DMA((2,)), pltpu.SemaphoreType.DMA((2,))],
        compiler_params=pltpu.CompilerParams(collective_id=1, has_side_effects=True),
        name="exchange_states",
    )(states)


def second_kernel(
    meta, states, mixed, halo, grad, weight, summed, q_i, k_i, tile_i, col_i, t_i, w_i, u_i, p_i, a_i,
    b_i, r_i, out_o, dmix_o, edge_o, back_o, taps_o, aux_o, st, rt, gs, cs,
):
    j = meta[0]
    ri, ci = iotas()
    rows = PER * L
    wq = weight[:, pl.ds(pl.multiple_of(j * DK, DK), DK)].astype(f32)
    wk = weight[:, pl.ds(pl.multiple_of((KH + j) * DK, DK), DK)].astype(f32)
    wv = weight[:, pl.ds(pl.multiple_of((2 * KH + 2 * j) * DK, 2 * DK), 2 * DK)].astype(f32)
    taps = jnp.concatenate([wq, wk, wv], axis=1)
    lower = jnp.where(ri >= ci, 1.0, 0.0).astype(f32)

    for h in range(2):
        st[h] = states[h]
        rt[2 * (NB - 1) + h] = states[2 + h]

    def scan(i, carry):
        m = NB - 1 - i
        for h in range(2):
            st[2 * (i + 1) + h] = (
                mm(split(st[2 * i + h]), split(a_i[2 * i + h]), NT) + b_i[2 * i + h]
            )

        @pl.when(m > 0)
        def _():
            for h in range(2):
                rt[2 * (m - 1) + h] = mm(split(rt[2 * m + h]), split(a_i[2 * m + h])) + r_i[2 * m + h]

        return carry

    lax.fori_loop(0, NB, scan, 0)

    gs[rows:, :] = jnp.zeros((8, 4 * DK), f32)
    cs[rows:, :] = jnp.full((8, 8), -2.0, f32)
    taps_o[...] = jnp.zeros((4, 4 * DK), f32)

    def body(step, carry):
        i = NB // PER - 1 - step
        r0 = pl.multiple_of(i * rows, rows)
        cs[0:rows, :] = col_i[pl.ds(pl.multiple_of(r0 + 8, 8), rows), :]
        sm = summed[pl.ds(r0, rows), :]
        sigma = 1.0 / (1.0 + jnp.exp(-sm))
        active = sm * sigma
        d_active = []
        for p in range(PER):
            lo = slice(p * L, (p + 1) * L)
            block = i * PER + p
            rb = pl.multiple_of(r0 + p * L, L)
            tile = tile_i[block]
            columns = cs[lo, :]
            doc_column = columns[:, 4:5]
            doc_before = col_i[pl.ds(pl.multiple_of(rb, 8), 8), :][7:8, 4:5]
            qb, kb = q_i[pl.ds(rb, L), :], k_i[pl.ds(rb, L), :]
            qs, ks = split(qb), split(kb)
            dq = jnp.zeros((L, DK), f32)
            dk = jnp.zeros((L, DK), f32)
            dvs = []
            small = jnp.zeros((L, L), f32)
            for h in range(2):
                n = 2 * block + h
                fade, enter, tail, keep, rate = gates(
                    tile, h, doc_column, tile[4:5, :], doc_before, columns
                )
                state = split(st[n])
                later = rt[n]
                laters = split(later)
                score = p_i[n]
                u = u_i[n] - mm(split(w_i[n]), state, NT)
                us = split(u)
                out = mm(split(enter * qb), state, NT) + mm(split(score), us)
                out_o[pl.ds(rb, L), h * DK : (h + 1) * DK] = out.astype(bf16)
                g = grad[pl.ds(rb, L), h * DK : (h + 1) * DK]
                gs1 = (g,)
                du = mm(split(jnp.transpose(score)), gs1) + mm(split(tail * kb), laters, NT)
                y = mm(split(jnp.transpose(t_i[n])), split(du))
                dv = rate * y
                d_score = mm(gs1, us, NT) * fade
                d_low = jnp.where(ri > ci, mm(split(y), us, NT) * (-rate * fade), 0.0)
                d_scores = split(d_score)
                dq = dq + enter * mm(gs1, state) + mm(d_scores, ks)
                dk = (
                    dk
                    - enter * mm(split(dv), state)
                    + mm(split(d_low + jnp.transpose(d_low)), ks)
                    + mm(split(jnp.transpose(d_score)), qs)
                    + tail * mm(us, laters)
                )
                v = active[lo, (2 + h) * DK : (3 + h) * DK]
                yu = y * u
                d_cum = jnp.sum(out * g.astype(f32) - v * dv, -1, keepdims=True)
                end = jnp.sum(jnp.sum(st[n + 2] * later, -1, keepdims=True), 0, keepdims=True)
                d_cum = d_cum + jnp.where(ri[:, 0:1] == L - 1, end, 0.0)
                d_rate = jnp.sum(yu, -1, keepdims=True) / rate
                small = small + jnp.where(ci == h, d_cum, 0.0) + jnp.where(ci == 2 + h, d_rate, 0.0)
                dvs.append(dv)
            small = jnp.transpose(small)[0:8, :]
            summed_back = exact(small, lower)
            which = lax.broadcasted_iota(jnp.int32, (8, 128), 0)
            aux_o[block] = jnp.where(which < 2, summed_back, small)
            d_active.append((dq, dk, dvs[0], dvs[1]))
        dq, dk, dv0, dv1 = (
            jnp.concatenate([d_active[p][c] for p in range(PER)], axis=0) for c in range(4)
        )
        aq, ak = active[:, :DK], active[:, DK : 2 * DK]
        nq = lax.rsqrt(jnp.sum(aq * aq, -1, keepdims=True) + EPS)
        nk = lax.rsqrt(jnp.sum(ak * ak, -1, keepdims=True) + EPS)
        dq = dq * DK**-0.5
        dq = nq * (dq - aq * (nq * nq * jnp.sum(aq * dq, -1, keepdims=True)))
        dk = nk * (dk - ak * (nk * nk * jnp.sum(ak * dk, -1, keepdims=True)))
        d_all = jnp.concatenate([dq, dk, dv0, dv1], axis=1)
        gs[0:rows, :] = d_all * (sigma * (1.0 + sm * (1.0 - sigma)))

        x = mixed[pl.ds(r0, rows), :].astype(f32)
        doc = cs[0:rows, 4:5]
        d_sum = gs[0:rows, :]
        dx = taps[3:4, :] * d_sum
        parts = [jnp.sum(d_sum * x, 0, keepdims=True)]
        for o in (1, 2, 3):
            moved = jnp.where(cs[o : o + rows, 4:5] == doc, gs[o : o + rows, :], 0.0)
            dx = dx + taps[3 - o : 4 - o, :] * moved
            parts.append(jnp.sum(moved * x, 0, keepdims=True))
        dmix_o[pl.ds(r0, rows), :] = dx.astype(bf16)

        @pl.when(step == 0)
        def _():
            edge_o[...] = dx[rows - 16 :, :]

        taps_o[...] = taps_o[...] + jnp.concatenate(parts[::-1], axis=0)
        gs[rows:, :] = gs[0:8, :]
        cs[rows:, :] = cs[0:8, :]
        return carry

    lax.fori_loop(0, NB // PER, body, 0)

    gs[0:8, :] = jnp.zeros((8, 4 * DK), f32)
    gs[8:16, :] = gs[rows:, :]
    cs[8:16, :] = cs[rows:, :]
    cs[0:8, :] = col_i[0:8, :]
    x = halo[8:16, :].astype(f32)
    dx = jnp.zeros((8, 4 * DK), f32)
    parts = [jnp.zeros((1, 4 * DK), f32)]
    for o in (1, 2, 3):
        moved = jnp.where(cs[o : o + 8, 4:5] == cs[0:8, 4:5], gs[o : o + 8, :], 0.0)
        dx = dx + taps[3 - o : 4 - o, :] * moved
        parts.append(jnp.sum(moved * x, 0, keepdims=True))
    taps_o[...] = taps_o[...] + jnp.concatenate(parts[::-1], axis=0)
    back_o[0:8, :] = jnp.zeros((8, 4 * DK), f32)
    back_o[8:16, :] = dx


def second_phase(meta, states, mixed, halo, grad, weight, kept, interpret=False):
    return pl.pallas_call(
        second_kernel,
        out_shape=(
            jax.ShapeDtypeStruct((QUARTER, 2 * DK), bf16),
            jax.ShapeDtypeStruct((QUARTER, 4 * DK), bf16),
            jax.ShapeDtypeStruct((16, 4 * DK), f32),
            jax.ShapeDtypeStruct((16, 4 * DK), f32),
            jax.ShapeDtypeStruct((4, 4 * DK), f32),
            jax.ShapeDtypeStruct((GROUP, 8, 128), f32),
        ),
        in_specs=[sspec] + [vspec] * 17,
        out_specs=(vspec,) * 6,
        scratch_shapes=[
            VM((2 * NB + 2, DK, DK), f32),
            VM((2 * NB, DK, DK), f32),
            VM((8 + PER * L, 4 * DK), f32),
            VM((8 + PER * L, 8), f32),
        ],
        compiler_params=pltpu.CompilerParams(vmem_limit_bytes=60 * 1024 * 1024),
        name="second_phase",
        interpret=interpret,
    )(meta, states, mixed, halo, grad, weight, *kept)


def tokens_kernel(
    out, dmix, edge, back, taps, aux, o_out, o_mix, o_taps, o_aux, part, total, gathered, edges,
    backs, send, recv, esend, erecv, bsend, brecv, tsend, trecv, gsend, grecv,
):
    dp = lax.axis_index("dp")
    me = lax.axis_index("seq")
    row, j = me // GROUP, lax.rem(me, GROUP)
    base = row * GROUP
    last = GROUP - 1
    before = lax.rem(row + 3, 4) * GROUP
    after = lax.rem(row + 1, 4) * GROUP
    is_last = j == last

    barrier = pltpu.get_barrier_semaphore()
    for s in range(1, GROUP):
        pl.semaphore_signal(
            barrier, inc=1, device_id=(dp, base + lax.rem(j + s, GROUP)), device_id_type=MESH
        )
    for n in range(1, 16):
        pl.semaphore_signal(
            barrier,
            inc=1,
            device_id=(lax.rem(dp + n // 4, 4), lax.rem(me + (n % 4) * GROUP, 4 * GROUP)),
            device_id_type=MESH,
        )

    @pl.when(is_last)
    def _():
        for to in range(GROUP):
            pl.semaphore_signal(barrier, inc=1, device_id=(dp, after + to), device_id_type=MESH)

    pl.semaphore_wait(barrier, GROUP - 1 + 15 + 1)

    def tap_copy(n):
        return pltpu.make_async_remote_copy(
            src_ref=taps.at[:, :],
            dst_ref=part.at[n],
            send_sem=tsend.at[n],
            recv_sem=trecv.at[n],
            device_id=(lax.rem(dp + n // 4, 4), lax.rem(me + (n % 4) * GROUP, 4 * GROUP)),
            device_id_type=MESH,
        )

    for n in range(1, 16):
        tap_copy(n).start()

    back_copy = pltpu.make_async_remote_copy(
        src_ref=back.at[:, :],
        dst_ref=backs.at[j],
        send_sem=bsend,
        recv_sem=brecv.at[j],
        device_id=(dp, before + last),
        device_id_type=MESH,
    )
    back_copy.start()

    def edge_copy():
        return pltpu.make_async_remote_copy(
            src_ref=edge.at[:, :],
            dst_ref=edges.at[j],
            send_sem=esend,
            recv_sem=erecv.at[j],
            device_id=(dp, base + last),
            device_id_type=MESH,
        )

    @pl.when(jnp.logical_not(is_last))
    def _():
        edge_copy().start()

    copies = []
    for s in range(1, GROUP):
        to = lax.rem(j + s, GROUP)
        r = pl.ds(pl.multiple_of(to * 128, 128), 128)
        two = pl.ds(pl.multiple_of(j * 2 * DK, 2 * DK), 2 * DK)
        pairs = (
            (out.at[r, :], o_out.at[:, two]),
            (dmix.at[r, pl.ds(0, DK)], o_mix.at[:, pl.ds(pl.multiple_of(j * DK, DK), DK)]),
            (
                dmix.at[r, pl.ds(DK, DK)],
                o_mix.at[:, pl.ds(pl.multiple_of((KH + j) * DK, DK), DK)],
            ),
            (
                dmix.at[r, pl.ds(2 * DK, 2 * DK)],
                o_mix.at[:, pl.ds(pl.multiple_of((2 * KH + 2 * j) * DK, 2 * DK), 2 * DK)],
            ),
            (aux.at[to], o_aux.at[j]),
        )
        for i, (src, dst) in enumerate(pairs):
            copy = pltpu.make_async_remote_copy(
                src_ref=src,
                dst_ref=dst,
                send_sem=send.at[s, i],
                recv_sem=recv.at[s, i],
                device_id=(dp, base + to),
                device_id_type=MESH,
            )
            copy.start()
            copies.append(copy)

    own = pl.ds(pl.multiple_of(j * 128, 128), 128)
    o_out[:, pl.ds(pl.multiple_of(j * 2 * DK, 2 * DK), 2 * DK)] = out[own, :]
    o_mix[:, pl.ds(pl.multiple_of(j * DK, DK), DK)] = dmix[own, 0:DK]
    o_mix[:, pl.ds(pl.multiple_of((KH + j) * DK, DK), DK)] = dmix[own, DK : 2 * DK]
    o_mix[:, pl.ds(pl.multiple_of((2 * KH + 2 * j) * DK, 2 * DK), 2 * DK)] = dmix[own, 2 * DK :]
    o_aux[j] = aux[j]

    for n in range(1, 16):
        tap_copy(n).wait_recv()
    whole = taps[...]
    for n in range(1, 16):
        whole = whole + part[n]
    total[...] = whole

    def gather_copy(s):
        return pltpu.make_async_remote_copy(
            src_ref=total.at[:, :],
            dst_ref=gathered.at[j],
            send_sem=gsend.at[s],
            recv_sem=grecv.at[s],
            device_id=(dp, base + lax.rem(j + s, GROUP)),
            device_id_type=MESH,
        )

    for s in range(1, GROUP):
        gather_copy(s).start()
    gathered[j] = whole

    for copy in copies:
        copy.wait()

    @pl.when(is_last)
    def _():
        edges[last] = edge[...]
        for src in range(GROUP):
            pltpu.make_async_remote_copy(
                src_ref=back.at[:, :],
                dst_ref=backs.at[src],
                send_sem=bsend,
                recv_sem=brecv.at[src],
                device_id=(dp, before + last),
                device_id_type=MESH,
            ).wait_recv()
        for src in range(GROUP - 1):
            pltpu.make_async_remote_copy(
                src_ref=edge.at[:, :],
                dst_ref=edges.at[src],
                send_sem=esend,
                recv_sem=erecv.at[src],
                device_id=(dp, base),
                device_id_type=MESH,
            ).wait_recv()
        for src in range(GROUP):
            fixed = (edges[src] + backs[src]).astype(bf16)
            o_mix[112:128, src * DK : (src + 1) * DK] = fixed[:, 0:DK]
            o_mix[112:128, (KH + src) * DK : (KH + src + 1) * DK] = fixed[:, DK : 2 * DK]
            o_mix[112:128, (2 * KH + 2 * src) * DK : (2 * KH + 2 * src + 2) * DK] = fixed[:, 2 * DK :]

    for s in range(1, GROUP):
        gather_copy(s).wait()
    for src in range(GROUP):
        o_taps[:, src * DK : (src + 1) * DK] = gathered[src][:, 0:DK]
        o_taps[:, (KH + src) * DK : (KH + src + 1) * DK] = gathered[src][:, DK : 2 * DK]
        o_taps[:, (2 * KH + 2 * src) * DK : (2 * KH + 2 * src + 2) * DK] = gathered[src][:, 2 * DK :]

    for n in range(1, 16):
        tap_copy(n).wait_send()
    back_copy.wait_send()

    @pl.when(jnp.logical_not(is_last))
    def _():
        edge_copy().wait_send()


def to_tokens(out, dmix, edge, back, taps, aux):
    dma = pltpu.SemaphoreType.DMA
    return pl.pallas_call(
        tokens_kernel,
        out_shape=(
            jax.ShapeDtypeStruct((128, 2 * KH * DK), bf16),
            jax.ShapeDtypeStruct((128, 4 * KH * DK), bf16),
            jax.ShapeDtypeStruct((4, 4 * KH * DK), f32),
            jax.ShapeDtypeStruct((GROUP, 8, 128), f32),
        ),
        in_specs=[vspec] * 6,
        out_specs=(vspec,) * 4,
        scratch_shapes=[
            VM((16, 4, 4 * DK), f32),
            VM((4, 4 * DK), f32),
            VM((GROUP, 4, 4 * DK), f32),
            VM((GROUP, 16, 4 * DK), f32),
            VM((GROUP, 16, 4 * DK), f32),
            dma((GROUP, 5)),
            dma((GROUP, 5)),
            dma,
            dma((GROUP,)),
            dma,
            dma((GROUP,)),
            dma((16,)),
            dma((16,)),
            dma((GROUP,)),
            dma((GROUP,)),
        ],
        compiler_params=pltpu.CompilerParams(collective_id=2, has_side_effects=True),
        name="to_tokens",
    )(out, dmix, edge, back, taps, aux)


def small_tiles(log_decay, beta, doc_ids):
    docs = jnp.broadcast_to(doc_ids.astype(f32)[None, None, :], (GROUP, 1, 128))
    return jnp.concatenate(
        [
            log_decay.reshape(GROUP, 2, 128),
            beta.reshape(GROUP, 2, 128),
            docs,
            jnp.zeros((GROUP, 3, 128), f32),
        ],
        axis=1,
    )


def local(mixed, conv_weight, log_decay, beta, doc_ids, out_grad):
    me = lax.axis_index("seq")
    meta = jnp.stack([lax.rem(me, GROUP), (me < GROUP).astype(jnp.int32)]).astype(jnp.int32)
    aux = small_tiles(log_decay[0], beta[0], doc_ids[0])
    rows, grad, aux_all, halo, halo_aux = to_heads(mixed[0], out_grad[0], aux)
    *kept, states = first_phase(meta, rows, halo, grad, aux_all, halo_aux, conv_weight)
    states = exchange_states(states)
    out, dmix, edge, back, taps, d_aux = second_phase(
        meta, states, rows, halo, grad, conv_weight, kept
    )
    out, dmix, taps, d_aux = to_tokens(out, dmix, edge, back, taps, d_aux)
    d_decay = d_aux[:, 0:2, :].reshape(VH, 128)
    d_beta = d_aux[:, 2:4, :].reshape(VH, 128)
    return out[None], dmix[None], taps, d_decay[None], d_beta[None]


def solution(mesh):
    in_specs = (
        P("dp", "seq", None),
        P(),
        P("dp", None, "seq"),
        P("dp", None, "seq"),
        P("dp", "seq"),
        P("dp", "seq", None),
    )
    out_specs = (
        P("dp", "seq", None),
        P("dp", "seq", None),
        P(),
        P("dp", None, "seq"),
        P("dp", None, "seq"),
    )
    return jax.shard_map(local, mesh=mesh, in_specs=in_specs, out_specs=out_specs, check_vma=False)
```

```python
import types

import jax
import jax.numpy as jnp
from jax import lax
from jax.experimental import pallas as pl
from jax.experimental.pallas import tpu as pltpu
from jax.sharding import PartitionSpec as P

DK = 128
KH = 8
VH = 16
L = 128
GROUP = 8
CHIPS = GROUP // 2
QUARTER = GROUP * 128
NB = QUARTER // L
PER = 2
ROWS = PER * L
EPS = 1e-6

f32 = jnp.float32
bf16 = jnp.bfloat16
NN = (((1,), (0,)), ((), ()))
NT = (((1,), (1,)), ((), ()))
MESH = pl.DeviceIdType.MESH
VM = pltpu.VMEM
vspec = pl.BlockSpec(memory_space=pltpu.VMEM)


def split(a):
    high = a.astype(bf16)
    return high, (a - high.astype(f32)).astype(bf16)


def stack(*pairs):
    return tuple(jnp.concatenate(x, axis=0) for x in zip(*pairs))


def mm(a, b, dims=NN):
    def dot(p, q):
        return lax.dot_general(p, q, dims, preferred_element_type=f32)

    if len(a) == 1:
        return dot(a[0], b[0]) + dot(a[0], b[1])
    rows = a[0].shape[0]
    both = dot(jnp.concatenate(a, axis=0), b[0])
    return both[:rows] + both[rows:] + dot(a[0], b[1])


def wide(a, b):
    left = jnp.concatenate([a[0], a[1], a[0]], axis=1)
    right = jnp.concatenate([b[0], b[0], b[1]], axis=0)
    return lax.dot_general(left, right, NN, preferred_element_type=f32)


def exact(a, b):
    return lax.dot_general(a, b, NN, preferred_element_type=f32, precision=lax.Precision.HIGHEST)


def iotas(rows=L):
    return (
        lax.broadcasted_iota(jnp.int32, (rows, L), 0),
        lax.broadcasted_iota(jnp.int32, (rows, L), 1),
    )


def invert(lows):
    ri, ci = iotas()
    eye = jnp.where(ri == ci, 1.0, 0.0).astype(f32)
    near = ri // 8 == ci // 8
    d = [jnp.where(near, x, 0.0) for x in lows]
    s1 = [split(x) for x in d]
    d2 = [mm(x, x) for x in s1]
    s2 = [split(x) for x in d2]
    d34 = [mm(stack(x, y), y) for x, y in zip(s1, s2)]
    inverse = [eye - x + y - z[:L] for x, y, z in zip(d, d2, d34)]
    inverse = [x + mm(split(x), split(z[L:])) for x, z in zip(inverse, d34)]
    half, lane = iotas(L // 2)
    size = 8
    while size < L:
        spots = range(0, L, 2 * size)
        mask = lane // size == 2 * (half // size)
        corner = [
            jnp.where(mask, jnp.concatenate([x[r + size : r + 2 * size] for r in spots], 0), 0.0)
            for x in lows
        ]
        inner = [mm(split(c), split(x)) for c, x in zip(corner, inverse)]
        zero = jnp.zeros((size, L), f32)
        spread = [
            jnp.concatenate(
                [p for m in range(len(spots)) for p in (zero, y[m * size : (m + 1) * size])], 0
            )
            for y in inner
        ]
        odd = [jnp.concatenate([x[r + size : r + 2 * size] for r in spots], 0) for x in inverse]
        odd = [x - mm(split(x), split(y)) for x, y in zip(odd, spread)]
        inverse = [
            jnp.concatenate(
                [
                    p
                    for m, r in enumerate(spots)
                    for p in (x[r : r + size], o[m * size : (m + 1) * size])
                ],
                0,
            )
            for x, o in zip(inverse, odd)
        ]
        size *= 2
    return inverse


def gates(tile, h, doc_column, doc_before, columns):
    ri, ci = iotas()
    doc_row = tile[4:5, :]
    cum = columns[:, h : h + 1]
    cum_row = tile[h : h + 1, :]
    doc_last = tile[4:5, L - 1 : L]
    cum_last = tile[h : h + 1, L - 1 : L]
    fade = jnp.where(
        (doc_column == doc_row) & (ri >= ci), jnp.exp(jnp.minimum(cum - cum_row, 0.0)), 0.0
    )
    enter = jnp.where(doc_column == doc_before, jnp.exp(cum), 0.0)
    return fade, enter, cum, cum_row, doc_row, doc_last, cum_last


def prepare_pair(e, i, first, taps):
    ri, ci = iotas()
    r0 = pl.multiple_of(i * ROWS, ROWS)
    e.xs[0:8, :] = e.halo[i][8:16, :].astype(f32)
    e.xs[8:, :] = e.rows[pl.ds(r0, ROWS), :].astype(f32)
    upper = jnp.where(ri <= ci, 1.0, 0.0).astype(f32)
    flat = jnp.concatenate([e.aux[PER * i + p] for p in range(PER)], axis=0)
    sums = exact(flat, upper)
    which = lax.rem(lax.broadcasted_iota(jnp.int32, (PER * 8, 128), 0), 8)
    flat = jnp.where(which < 2, sums, flat)
    tiles = [flat[8 * p : 8 * p + 8] for p in range(PER)]
    edge_columns = jnp.transpose(e.haux[i])[120:128, :]
    at_start = (first + (i == 0).astype(jnp.int32)) == 2
    e.ds[0:8, :] = jnp.where(at_start, -1.0, edge_columns)
    for p in range(PER):
        e.tile[PER * i + p] = tiles[p]
        e.ds[8 + p * L : 8 + (p + 1) * L, :] = jnp.transpose(tiles[p])
    e.col[i] = e.ds[...]
    doc = e.ds[8:, 4:5]
    summed = taps[3:4, :] * e.xs[8:, :]
    for o in (1, 2, 3):
        same = e.ds[8 - o : 8 - o + ROWS, 4:5] == doc
        summed = summed + taps[3 - o : 4 - o, :] * jnp.where(
            same, e.xs[8 - o : 8 - o + ROWS, :], 0.0
        )
    e.summed[pl.ds(r0, ROWS), :] = summed
    active = summed / (1.0 + jnp.exp(-summed))
    q = active[:, :DK]
    k = active[:, DK : 2 * DK]
    q = q * lax.rsqrt(jnp.sum(q * q, -1, keepdims=True) + EPS) * DK**-0.5
    k = k * lax.rsqrt(jnp.sum(k * k, -1, keepdims=True) + EPS)
    e.q[pl.ds(r0, ROWS), :] = q
    e.k[pl.ds(r0, ROWS), :] = k

    chains = []
    for p in range(PER):
        lo = slice(p * L, (p + 1) * L)
        kp, qp = k[lo], q[lo]
        ks = split(kp)
        both = mm(stack(ks, split(qp)), ks, NT)
        inner, score = both[:L], both[L:]
        columns = e.ds[8 + p * L : 8 + (p + 1) * L, :]
        doc_before = e.ds[7 + p * L : 8 + p * L, 4:5]
        turned = jnp.transpose(kp)
        for h in range(2):
            fade, enter, cum, cum_row, doc_row, doc_last, cum_last = gates(
                tiles[p], h, columns[:, 4:5], doc_before, columns
            )
            rate = columns[:, 2 + h : 3 + h]
            tail_row = jnp.where(doc_row == doc_last, jnp.exp(cum_last - cum_row), 0.0)
            keep = jnp.where(doc_last == doc_before, jnp.exp(cum_last), 0.0)
            chains.append(
                dict(
                    n=(PER * i + p) * 2 + h,
                    low=jnp.where(ri > ci, rate * inner * fade, 0.0),
                    left=jnp.concatenate([score * fade, turned * tail_row], axis=0),
                    right=jnp.concatenate(
                        [(rate * enter) * kp, rate * active[lo, (2 + h) * DK : (3 + h) * DK]], axis=1
                    ),
                    eq=enter * qp,
                    keep=keep,
                )
            )
    inverse = invert([c["low"] for c in chains])
    for c, t in zip(chains, inverse):
        n = c["n"]
        ts = split(t)
        ns = split(mm(split(c["left"]), ts))
        e.nh[n] = ns[0]
        e.nl[n] = ns[1]
        big = wide(stack(ts, ns), split(c["right"]))
        ws = split(jnp.concatenate([big[:L, :DK], c["eq"] - big[L : 2 * L, :DK]], axis=0))
        e.wh[n] = ws[0]
        e.wl[n] = ws[1]
        e.u[n] = big[:L, DK:]
        e.o[n] = big[L : 2 * L, DK:]
        a = split(jnp.where(ri == ci, c["keep"], 0.0) - big[2 * L :, :DK])
        e.ah[n] = a[0]
        e.al[n] = a[1]
        e.b[n] = big[2 * L :, DK:]


def backward_terms(e, i):
    for p in range(PER):
        rb = pl.multiple_of(i * ROWS + p * L, L)
        for h in range(2):
            n = (PER * i + p) * 2 + h
            g = e.grad[pl.ds(rb, L), h * DK : (h + 1) * DK]
            turned = jnp.transpose(g.astype(f32)).astype(bf16)
            e.gt[n] = turned
            e.r[n] = mm((turned,), (e.wh[n][L:], e.wl[n][L:]))


def scans(e):
    def step(i, carry):
        m = NB - 1 - i
        for h in range(2):
            n = 2 * i + h
            e.st[n + 2] = mm((e.ah[n], e.al[n]), split(e.st[n])) + e.b[n]
        for h in range(2):
            n = 2 * m + h
            e.rt[n] = mm(split(e.rt[n + 2]), (e.ah[n], e.al[n])) + e.r[n]
        return carry

    lax.fori_loop(0, NB, step, 0)


def finish_pair(e, i, t, taps):
    ri, ci = iotas()
    lower = jnp.where(ri >= ci, 1.0, 0.0).astype(f32)
    r0 = pl.multiple_of(i * ROWS, ROWS)
    e.cs[0 : 8 + ROWS, :] = e.col[i]
    sm = e.summed[pl.ds(r0, ROWS), :]
    sigma = 1.0 / (1.0 + jnp.exp(-sm))
    active = sm * sigma
    pieces = []
    for p in range(PER):
        lo = slice(p * L, (p + 1) * L)
        block = PER * i + p
        rb = pl.multiple_of(r0 + p * L, L)
        tile = e.tile[block]
        columns = e.cs[8 + p * L : 8 + (p + 1) * L, :]
        doc_before = e.cs[7 + p * L : 8 + p * L, 4:5]
        d_score = jnp.zeros((L, L), f32)
        d_low = jnp.zeros((L, L), f32)
        dq = jnp.zeros((L, DK), f32)
        dk = jnp.zeros((L, DK), f32)
        small = jnp.zeros((L, L), f32)
        dvs, ends = [], []
        for h in range(2):
            n = 2 * block + h
            fade, enter, cum, cum_row, doc_row, doc_last, cum_last = gates(
                tile, h, columns[:, 4:5], doc_before, columns
            )
            rate = columns[:, 2 + h : 3 + h]
            tail = jnp.where(columns[:, 4:5] == doc_last, jnp.exp(cum_last - cum), 0.0)
            state = split(e.st[n])
            later = e.rt[n + 2]
            laters = split(later)
            both = mm((e.wh[n], e.wl[n]), state)
            u = e.u[n] - both[:L]
            out = e.o[n] + both[L:]
            e.out[pl.ds(rb, L), h * DK : (h + 1) * DK] = out.astype(bf16)
            g = e.grad[pl.ds(rb, L), h * DK : (h + 1) * DK]
            ns = (e.nh[n], e.nl[n])
            yt = mm((e.gt[n],), (ns[0][:L], ns[1][:L])) + mm(laters, (ns[0][L:], ns[1][L:]))
            y = jnp.transpose(yt)
            ys = split(y)
            us = split(u)
            right = stack(us, state)
            tops = jnp.concatenate([g, ys[0], ys[1]], axis=0)

            def dot(a, b):
                return lax.dot_general(a, b, NT, preferred_element_type=f32)

            res = dot(tops, right[0])
            fine = dot(tops[: 2 * L], right[1])
            gu = res[:L] + fine[:L]
            yu = res[L : 2 * L] + res[2 * L :] + fine[L:]
            d_score = d_score + gu[:, :L] * fade
            d_low = d_low - jnp.where(ri > ci, yu[:, :L] * (rate * fade), 0.0)
            dq = dq + enter * gu[:, L:]
            dk = dk - (enter * rate) * yu[:, L:]
            dv = rate * y
            dvs.append(dv)
            ends.append((us, tail, laters))
            v = active[lo, (2 + h) * DK : (3 + h) * DK]
            d_cum = jnp.sum(out * g.astype(f32) - v * dv, -1, keepdims=True)
            end = jnp.sum(e.st[n + 2] * jnp.transpose(later), -1, keepdims=True)
            end = jnp.sum(end, 0, keepdims=True)
            d_cum = d_cum + jnp.where(ri[:, 0:1] == L - 1, end, 0.0)
            d_rate = jnp.sum(y * u, -1, keepdims=True) / rate
            small = small + jnp.where(ci == h, d_cum, 0.0) + jnp.where(ci == 2 + h, d_rate, 0.0)
        ks = split(e.k[pl.ds(rb, L), :])
        qs = split(e.q[pl.ds(rb, L), :])
        both = mm(split(jnp.concatenate([d_score, d_low + jnp.transpose(d_low)], axis=0)), ks)
        dq = dq + both[:L]
        dk = dk + both[L:] + mm(split(jnp.transpose(d_score)), qs)
        for us, tail, laters in ends:
            dk = dk + tail * mm(us, laters)
        small = jnp.transpose(small)[0:8, :]
        which = lax.broadcasted_iota(jnp.int32, (8, 128), 0)
        e.daux[block] = jnp.where(which < 2, exact(small, lower), small)
        pieces.append((dq, dk, dvs[0], dvs[1]))
    dq, dk, dv0, dv1 = (jnp.concatenate(x, axis=0) for x in zip(*pieces))
    aq, ak = active[:, :DK], active[:, DK : 2 * DK]
    nq = lax.rsqrt(jnp.sum(aq * aq, -1, keepdims=True) + EPS)
    nk = lax.rsqrt(jnp.sum(ak * ak, -1, keepdims=True) + EPS)
    dq = dq * DK**-0.5
    dq = nq * (dq - aq * (nq * nq * jnp.sum(aq * dq, -1, keepdims=True)))
    dk = nk * (dk - ak * (nk * nk * jnp.sum(ak * dk, -1, keepdims=True)))
    d_all = jnp.concatenate([dq, dk, dv0, dv1], axis=1)
    d_sum = d_all * (sigma * (1.0 + sm * (1.0 - sigma)))
    e.gs[8 : 8 + ROWS, :] = d_sum

    x = e.rows[pl.ds(r0, ROWS), :].astype(f32)
    doc = e.cs[8 : 8 + ROWS, 4:5]
    before = e.cs[0:8, 4:5]
    xh = e.halo[i][8:16, :].astype(f32)
    dx = taps[3:4, :] * d_sum
    back = jnp.zeros((8, 4 * DK), f32)
    parts = [jnp.sum(d_sum * x, 0, keepdims=True)]
    for o in (1, 2, 3):
        tap = taps[3 - o : 4 - o, :]
        moved = jnp.where(
            e.cs[8 + o : 8 + o + ROWS, 4:5] == doc, e.gs[8 + o : 8 + o + ROWS, :], 0.0
        )
        dx = dx + tap * moved
        over = jnp.where(e.cs[o : o + 8, 4:5] == before, e.gs[o : o + 8, :], 0.0)
        back = back + tap * over
        parts.append(
            jnp.sum(moved * x, 0, keepdims=True) + jnp.sum(over * xh, 0, keepdims=True)
        )
    e.dmix[pl.ds(r0, ROWS), :] = dx.astype(bf16)
    e.edge[t] = dx[ROWS - 8 :, :]
    e.back[t] = back
    e.taps[...] = e.taps[...] + jnp.concatenate(parts[::-1], axis=0)


def start_finish(e):
    e.gs[0:8, :] = jnp.zeros((8, 4 * DK), f32)
    e.gs[8 + ROWS :, :] = jnp.zeros((8, 4 * DK), f32)
    e.cs[8 + ROWS :, :] = jnp.full((8, 8), -2.0, f32)
    e.taps[...] = jnp.zeros((4, 4 * DK), f32)


def head_taps(weight, j):
    wq = weight[:, pl.ds(pl.multiple_of(j * DK, DK), DK)]
    wk = weight[:, pl.ds(pl.multiple_of((KH + j) * DK, DK), DK)]
    wv = weight[:, pl.ds(pl.multiple_of((2 * KH + 2 * j) * DK, 2 * DK), 2 * DK)]
    return jnp.concatenate([wq.astype(f32), wk.astype(f32), wv.astype(f32)], axis=1)


SQ = (2 * NB, DK, DK)
SCRATCH = dict(
    rows=((QUARTER, 4 * DK), bf16),
    grad=((QUARTER, 2 * DK), bf16),
    aux=((GROUP, 8, 128), f32),
    halo=((CHIPS, 16, 4 * DK), bf16),
    haux=((CHIPS, 8, 128), f32),
    xs=((8 + ROWS, 4 * DK), f32),
    ds=((8 + ROWS, 8), f32),
    tile=((NB, 8, 128), f32),
    col=((CHIPS, 8 + ROWS, 8), f32),
    summed=((QUARTER, 4 * DK), f32),
    q=((QUARTER, DK), f32),
    k=((QUARTER, DK), f32),
    nh=((2 * NB, 2 * L, L), bf16),
    nl=((2 * NB, 2 * L, L), bf16),
    wh=((2 * NB, 2 * L, DK), bf16),
    wl=((2 * NB, 2 * L, DK), bf16),
    ah=(SQ, bf16),
    al=(SQ, bf16),
    u=(SQ, f32),
    o=(SQ, f32),
    b=(SQ, f32),
    r=(SQ, f32),
    gt=(SQ, bf16),
    st=((2 * NB + 2, DK, DK), f32),
    rt=((2 * NB + 2, DK, DK), f32),
    cs=((16 + ROWS, 8), f32),
    gs=((16 + ROWS, 4 * DK), f32),
    out=((QUARTER, 2 * DK), bf16),
    dmix=((QUARTER, 4 * DK), bf16),
    edge=((CHIPS, 8, 4 * DK), f32),
    back=((CHIPS, 8, 4 * DK), f32),
    taps=((4, 4 * DK), f32),
    daux=((GROUP, 8, 128), f32),
)


ARGS = ("mixed", "weight", "decay", "rate", "docs", "grad_in")
OUTS = ("o_out", "o_mix", "o_taps", "o_decay", "o_rate")
EXTRA = dict(
    aux_own=((GROUP, 8, 128), f32),
    arrived=((4, DK, DK), f32),
    edges=((GROUP, 8, 4 * DK), f32),
    backs=((GROUP, 8, 4 * DK), f32),
    part=((16, 4, 4 * DK), f32),
    total=((4, 4 * DK), f32),
    gathered=((GROUP, 4, 4 * DK), f32),
    daux_in=((GROUP, 8, 128), f32),
)
SEMS = dict(
    asend=(GROUP, 5),
    arecv=(GROUP, 5),
    hsend=(GROUP, 4),
    hrecv=(CHIPS, 4),
    ssend=(2,),
    srecv=(2,),
    bsend=(CHIPS,),
    brecv=(GROUP,),
    esend=(CHIPS,),
    erecv=(GROUP,),
    fsend=(GROUP, 5),
    frecv=(GROUP, 5),
    tsend=(16,),
    trecv=(16,),
    gsend=(GROUP,),
    grecv=(GROUP,),
)
NAMES = ARGS + OUTS + tuple(SCRATCH) + tuple(EXTRA) + tuple(SEMS)


def head_columns(to):
    return (
        pl.ds(pl.multiple_of(to * DK, DK), DK),
        pl.ds(pl.multiple_of((KH + to) * DK, DK), DK),
        pl.ds(pl.multiple_of((2 * KH + 2 * to) * DK, 2 * DK), 2 * DK),
    )


OWN = (pl.ds(0, DK), pl.ds(DK, DK), pl.ds(2 * DK, 2 * DK))


def two_columns(to):
    return pl.ds(pl.multiple_of(to * 2 * DK, 2 * DK), 2 * DK)


def place(j):
    return pl.ds(pl.multiple_of(j * 128, 128), 128)


def layer_kernel(*refs):
    e = types.SimpleNamespace(**dict(zip(NAMES, refs)))
    dp = lax.axis_index("dp")
    me = lax.axis_index("seq")
    row, j = me // GROUP, lax.rem(me, GROUP)
    y, c = j // 2, lax.rem(j, 2)
    base = row * GROUP
    last = GROUP - 1
    before = lax.rem(row + 3, 4) * GROUP
    after = lax.rem(row + 1, 4) * GROUP
    is_last = j == last
    first = (row == 0).astype(jnp.int32)

    def remote(src, dst, send, recv, seq, slab=None):
        return pltpu.make_async_remote_copy(
            src_ref=src,
            dst_ref=dst,
            send_sem=send,
            recv_sem=recv,
            device_id=(dp if slab is None else slab, seq),
            device_id_type=MESH,
        )

    def peer(dy, dc):
        return 2 * lax.rem(y + dy, CHIPS) + lax.rem(c + dc, 2)

    def plane(n):
        return lax.rem(dp + n // 4, 4), lax.rem(me + (n % 4) * GROUP, 4 * GROUP)

    barrier = pltpu.get_barrier_semaphore()

    def greet(slab, seq):
        pl.semaphore_signal(barrier, inc=1, device_id=(slab, seq), device_id_type=MESH)

    for s in range(1, GROUP):
        greet(dp, base + lax.rem(j + s, GROUP))
    for n in range(1, 16):
        greet(*plane(n))
    greet(dp, before + last)

    @pl.when(is_last)
    def _():
        for to in range(GROUP):
            greet(dp, after + to)

    docs = e.docs[...].astype(f32)
    for to in range(GROUP):
        e.aux_own[to] = jnp.concatenate(
            [
                e.decay[2 * to : 2 * to + 2, :],
                e.rate[2 * to : 2 * to + 2, :],
                docs,
                jnp.zeros((3, 128), f32),
            ],
            axis=0,
        )
    taps = head_taps(e.weight, j)
    pl.semaphore_wait(barrier, jnp.where(is_last, GROUP - 1 + 15 + 1 + GROUP, GROUP - 1 + 15 + 1))

    slot = lax.rem(y + 1, CHIPS)
    inside = y < CHIPS - 1
    there = jnp.where(inside, base, after)

    def halo_copies(to, at, group):
        own = head_columns(to)
        r = pl.ds(112, 16)
        pairs = [(e.mixed.at[r, own[n]], e.halo.at[at, :, OWN[n]]) for n in range(3)]
        pairs.append((e.aux_own.at[to], e.haux.at[at]))
        return [
            remote(src, dst, e.hsend.at[to, n], e.hrecv.at[at, n], group + to)
            for n, (src, dst) in enumerate(pairs)
        ]

    @pl.when(c == 1)
    def _():
        for to in range(GROUP):

            @pl.when(jnp.logical_not(inside) | (j != to))
            def _():
                for copy in halo_copies(to, slot, there):
                    copy.start()

        @pl.when(inside)
        def _():
            own = head_columns(j)
            for n in range(3):
                e.halo[slot, :, OWN[n]] = e.mixed[112:128, own[n]]
            e.haux[slot] = e.aux_own[j]

    def dy_of(t):
        return t + t // 2 - 2 * (t // 3)

    def head_copy(t, dc, n):
        to = peer(dy_of(t), dc)
        own = head_columns(to)
        at = place(j)
        src, dst = (
            (e.mixed.at[:, own[0]], e.rows.at[at, OWN[0]]),
            (e.mixed.at[:, own[1]], e.rows.at[at, OWN[1]]),
            (e.mixed.at[:, own[2]], e.rows.at[at, OWN[2]]),
            (e.aux_own.at[to], e.aux.at[j]),
            (e.grad_in.at[:, two_columns(to)], e.grad.at[at, :]),
        )[n]
        k = 2 * t + dc
        return remote(src, dst, e.asend.at[k, n], e.arecv.at[k, n], base + to)

    steps = [(t, dc) for t in range(CHIPS) for dc in range(2) if (t, dc) != (0, 0)]
    for t, dc in steps:
        for n in range(4):
            head_copy(t, dc, n).start()
    for t, dc in steps:
        head_copy(t, dc, 4).start()

    own = head_columns(j)
    for n in range(3):
        e.rows[place(j), OWN[n]] = e.mixed[:, own[n]]
    e.aux[j] = e.aux_own[j]
    e.grad[place(j), :] = e.grad_in[:, two_columns(j)]

    def pair_of(t):
        return lax.rem(y + CHIPS - dy_of(t), CHIPS)

    def prepare(t, carry):
        i = pair_of(t)

        @pl.when(t > 0)
        def _():
            for n in range(4):
                head_copy(t, 0, n).wait_recv()

        for n in range(4):
            head_copy(t, 1, n).wait_recv()

        @pl.when((i == 0) | (2 * i - 1 != j))
        def _():
            for copy in halo_copies(0, i, base):
                copy.wait_recv()

        prepare_pair(e, i, first, taps)
        return carry

    lax.fori_loop(0, CHIPS, prepare, 0)

    def turn(t, carry):
        @pl.when(t > 0)
        def _():
            head_copy(t, 0, 4).wait_recv()

        head_copy(t, 1, 4).wait_recv()
        backward_terms(e, pair_of(t))
        return carry

    lax.fori_loop(0, CHIPS, turn, 0)

    zero = jnp.zeros((2, DK, DK), f32)
    e.st[0:2] = zero
    e.rt[2 * NB :] = zero
    scans(e)
    start_finish(e)
    hops = (
        remote(
            e.st.at[pl.ds(2 * NB, 2)],
            e.arrived.at[pl.ds(0, 2)],
            e.ssend.at[0],
            e.srecv.at[0],
            lax.rem(me + GROUP, 4 * GROUP),
        ),
        remote(
            e.rt.at[pl.ds(0, 2)],
            e.arrived.at[pl.ds(2, 2)],
            e.ssend.at[1],
            e.srecv.at[1],
            lax.rem(me + 3 * GROUP, 4 * GROUP),
        ),
    )
    for copy in hops:
        copy.start()
    for t, dc in steps:
        for n in range(5):
            head_copy(t, dc, n).wait_send()

    @pl.when(c == 1)
    def _():
        for to in range(GROUP):

            @pl.when(jnp.logical_not(inside) | (j != to))
            def _():
                for copy in halo_copies(to, slot, there):
                    copy.wait_send()

    for copy in hops:
        copy.wait()
    e.st[0:2] = e.arrived[0:2]
    e.rt[2 * NB :] = e.arrived[2:4]
    scans(e)

    def token_copies(t, dc):
        to = peer(t + 1, dc)
        r = place(to)
        own = head_columns(j)
        pairs = [(e.out.at[r, :], e.o_out.at[:, two_columns(j)])]
        pairs += [(e.dmix.at[r, OWN[n]], e.o_mix.at[:, own[n]]) for n in range(3)]
        pairs.append((e.daux.at[to], e.daux_in.at[j]))
        k = 2 * t + dc
        return [
            remote(src, dst, e.fsend.at[k, n], e.frecv.at[k, n], base + to)
            for n, (src, dst) in enumerate(pairs)
        ]

    def edge_copy(i, at):
        return remote(
            e.edge.at[at], e.edges.at[j], e.esend.at[at], e.erecv.at[j], base + 2 * i + 1
        )

    def back_copy(i, at):
        to = jnp.where(i == 0, before + last, base + 2 * i - 1)
        return remote(e.back.at[at], e.backs.at[j], e.bsend.at[at], e.brecv.at[j], to)

    def finish(t, carry):
        i = lax.rem(y + t + 1, CHIPS)
        finish_pair(e, i, t, taps)

        @pl.when(t < CHIPS - 1)
        def _():
            for copy in token_copies(t, 0):
                copy.start()

        for copy in token_copies(t, 1):
            copy.start()

        @pl.when(2 * i + 1 == j)
        def _():
            e.edges[j] = e.edge[t]

        @pl.when(2 * i + 1 != j)
        def _():
            edge_copy(i, t).start()

        @pl.when((i > 0) & (2 * i - 1 == j))
        def _():
            e.backs[j] = e.back[t]

        @pl.when((i == 0) | (2 * i - 1 != j))
        def _():
            back_copy(i, t).start()

        return carry

    lax.fori_loop(0, CHIPS, finish, 0)

    spot = 4 * dp + row

    def tap_copy(n):
        slab, seq = plane(n)
        return remote(e.taps.at[:, :], e.part.at[spot], e.tsend.at[n], e.trecv.at[n], seq, slab)

    for n in range(1, 16):
        tap_copy(n).start()

    own = head_columns(j)
    e.o_out[:, two_columns(j)] = e.out[place(j), :]
    for n in range(3):
        e.o_mix[:, own[n]] = e.dmix[place(j), OWN[n]]
    e.daux_in[j] = e.daux[j]

    for n in range(1, 16):
        tap_copy(n).wait_recv()
    e.part[spot] = e.taps[...]
    whole = e.part[0]
    for n in range(1, 16):
        whole = whole + e.part[n]
    e.total[...] = whole
    e.gathered[j] = whole

    def gather_copy(s):
        return remote(
            e.total.at[:, :],
            e.gathered.at[j],
            e.gsend.at[s],
            e.grecv.at[s],
            base + lax.rem(j + s, GROUP),
        )

    for s in range(1, GROUP):
        gather_copy(s).start()

    for t in range(CHIPS):
        for dc in range(2):
            if (t, dc) != (CHIPS - 1, 0):
                for copy in token_copies(t, dc):
                    copy.wait()

    @pl.when(c == 1)
    def _():
        for src in range(GROUP):

            def edge_from():
                return remote(
                    e.edge.at[0], e.edges.at[src], e.esend.at[0], e.erecv.at[src], base + last
                )

            def back_from():
                return remote(
                    e.back.at[0], e.backs.at[src], e.bsend.at[0], e.brecv.at[src], base + last
                )

            @pl.when(j != src)
            def _():
                edge_from().wait_recv()

            @pl.when(jnp.logical_not(inside) | (j != src))
            def _():
                back_from().wait_recv()

        for src in range(GROUP):
            fixed = e.edges[src] + e.backs[src]
            spots = (
                (src * DK, DK, 0),
                ((KH + src) * DK, DK, DK),
                ((2 * KH + 2 * src) * DK, 2 * DK, 2 * DK),
            )
            for at, width, own_at in spots:
                old = e.o_mix[112:128, at : at + width].astype(f32)
                new = jnp.concatenate([old[0:8], fixed[:, own_at : own_at + width]], axis=0)
                e.o_mix[112:128, at : at + width] = new.astype(bf16)

    for src in range(GROUP):
        e.o_decay[2 * src : 2 * src + 2, :] = e.daux_in[src][0:2, :]
        e.o_rate[2 * src : 2 * src + 2, :] = e.daux_in[src][2:4, :]

    for s in range(1, GROUP):
        gather_copy(s).wait()
    for src in range(GROUP):
        got = e.gathered[src]
        e.o_taps[:, src * DK : (src + 1) * DK] = got[:, 0:DK]
        e.o_taps[:, (KH + src) * DK : (KH + src + 1) * DK] = got[:, DK : 2 * DK]
        e.o_taps[:, (2 * KH + 2 * src) * DK : (2 * KH + 2 * src + 2) * DK] = got[:, 2 * DK :]

    for n in range(1, 16):
        tap_copy(n).wait_send()
    for t in range(CHIPS):
        i = lax.rem(y + t + 1, CHIPS)

        @pl.when(2 * i + 1 != j)
        def _():
            edge_copy(i, t).wait_send()

        @pl.when((i == 0) | (2 * i - 1 != j))
        def _():
            back_copy(i, t).wait_send()


def layer(*args):
    scratch = [VM(*x) for x in SCRATCH.values()] + [VM(*x) for x in EXTRA.values()]
    return pl.pallas_call(
        layer_kernel,
        out_shape=(
            jax.ShapeDtypeStruct((128, 2 * KH * DK), bf16),
            jax.ShapeDtypeStruct((128, 4 * KH * DK), bf16),
            jax.ShapeDtypeStruct((4, 4 * KH * DK), f32),
            jax.ShapeDtypeStruct((VH, 128), f32),
            jax.ShapeDtypeStruct((VH, 128), f32),
        ),
        in_specs=[vspec] * len(ARGS),
        out_specs=(vspec,) * len(OUTS),
        scratch_shapes=scratch + [pltpu.SemaphoreType.DMA(x) for x in SEMS.values()],
        compiler_params=pltpu.CompilerParams(
            collective_id=0, has_side_effects=True, vmem_limit_bytes=60 * 1024 * 1024
        ),
        name="layer",
    )(*args)


def local(mixed, conv_weight, log_decay, beta, doc_ids, out_grad):
    out, dmix, taps, d_decay, d_beta = layer(
        mixed[0], conv_weight, log_decay[0], beta[0], doc_ids, out_grad[0]
    )
    return out[None], dmix[None], taps, d_decay[None], d_beta[None]


def solution(mesh):
    in_specs = (
        P("dp", "seq", None),
        P(),
        P("dp", None, "seq"),
        P("dp", None, "seq"),
        P("dp", "seq"),
        P("dp", "seq", None),
    )
    out_specs = (
        P("dp", "seq", None),
        P("dp", "seq", None),
        P(),
        P("dp", None, "seq"),
        P("dp", None, "seq"),
    )
    return jax.shard_map(local, mesh=mesh, in_specs=in_specs, out_specs=out_specs, check_vma=False)
```

```python
import types

import jax
import jax.numpy as jnp
from jax import lax
from jax.experimental import pallas as pl
from jax.experimental.pallas import tpu as pltpu
from jax.sharding import PartitionSpec as P

DK = 128
KH = 8
VH = 16
L = 128
GROUP = 8
CHIPS = GROUP // 2
QUARTER = GROUP * 128
NB = QUARTER // L
PER = 2
ROWS = PER * L
EPS = 1e-6

f32 = jnp.float32
bf16 = jnp.bfloat16
NN = (((1,), (0,)), ((), ()))
NT = (((1,), (1,)), ((), ()))
MESH = pl.DeviceIdType.MESH
VM = pltpu.VMEM
vspec = pl.BlockSpec(memory_space=pltpu.VMEM)


def split(a):
    high = a.astype(bf16)
    return high, (a - high.astype(f32)).astype(bf16)


def stack(*pairs):
    return tuple(jnp.concatenate(x, axis=0) for x in zip(*pairs))


def mm(a, b, dims=NN):
    def dot(p, q):
        return lax.dot_general(p, q, dims, preferred_element_type=f32)

    if len(a) == 1:
        return dot(a[0], b[0]) + dot(a[0], b[1])
    rows = a[0].shape[0]
    both = dot(jnp.concatenate(a, axis=0), b[0])
    return both[:rows] + both[rows:] + dot(a[0], b[1])


def wide(a, b):
    left = jnp.concatenate([a[0], a[1], a[0]], axis=1)
    right = jnp.concatenate([b[0], b[0], b[1]], axis=0)
    return lax.dot_general(left, right, NN, preferred_element_type=f32)


def exact(a, b):
    return lax.dot_general(a, b, NN, preferred_element_type=f32, precision=lax.Precision.HIGHEST)


def iotas(rows=L):
    return (
        lax.broadcasted_iota(jnp.int32, (rows, L), 0),
        lax.broadcasted_iota(jnp.int32, (rows, L), 1),
    )


def invert(lows):
    ri, ci = iotas()
    eye = jnp.where(ri == ci, 1.0, 0.0).astype(f32)
    near = ri // 8 == ci // 8
    d = [jnp.where(near, x, 0.0) for x in lows]
    s1 = [split(x) for x in d]
    d2 = [mm(x, x) for x in s1]
    s2 = [split(x) for x in d2]
    d34 = [mm(stack(x, y), y) for x, y in zip(s1, s2)]
    inverse = [eye - x + y - z[:L] for x, y, z in zip(d, d2, d34)]
    inverse = [x + mm(split(x), split(z[L:])) for x, z in zip(inverse, d34)]
    half, lane = iotas(L // 2)
    size = 8
    while size < L:
        spots = range(0, L, 2 * size)
        mask = lane // size == 2 * (half // size)
        corner = [
            jnp.where(mask, jnp.concatenate([x[r + size : r + 2 * size] for r in spots], 0), 0.0)
            for x in lows
        ]
        inner = [mm(split(c), split(x)) for c, x in zip(corner, inverse)]
        zero = jnp.zeros((size, L), f32)
        spread = [
            jnp.concatenate(
                [p for m in range(len(spots)) for p in (zero, y[m * size : (m + 1) * size])], 0
            )
            for y in inner
        ]
        odd = [jnp.concatenate([x[r + size : r + 2 * size] for r in spots], 0) for x in inverse]
        odd = [x - mm(split(x), split(y)) for x, y in zip(odd, spread)]
        inverse = [
            jnp.concatenate(
                [
                    p
                    for m, r in enumerate(spots)
                    for p in (x[r : r + size], o[m * size : (m + 1) * size])
                ],
                0,
            )
            for x, o in zip(inverse, odd)
        ]
        size *= 2
    return inverse


def gates(tile, h, doc_column, doc_before, columns):
    ri, ci = iotas()
    doc_row = tile[4:5, :]
    cum = columns[:, h : h + 1]
    cum_row = tile[h : h + 1, :]
    doc_last = tile[4:5, L - 1 : L]
    cum_last = tile[h : h + 1, L - 1 : L]
    fade = jnp.where(
        (doc_column == doc_row) & (ri >= ci), jnp.exp(jnp.minimum(cum - cum_row, 0.0)), 0.0
    )
    enter = jnp.where(doc_column == doc_before, jnp.exp(cum), 0.0)
    return fade, enter, cum, cum_row, doc_row, doc_last, cum_last


def prepare_pair(e, i, first, taps):
    ri, ci = iotas()
    r0 = pl.multiple_of(i * ROWS, ROWS)
    e.xs[0:8, :] = e.halo[i][8:16, :].astype(f32)
    e.xs[8:, :] = e.rows[pl.ds(r0, ROWS), :].astype(f32)
    upper = jnp.where(ri <= ci, 1.0, 0.0).astype(f32)
    flat = jnp.concatenate([e.aux[PER * i + p] for p in range(PER)], axis=0)
    sums = exact(flat, upper)
    which = lax.rem(lax.broadcasted_iota(jnp.int32, (PER * 8, 128), 0), 8)
    flat = jnp.where(which < 2, sums, flat)
    tiles = [flat[8 * p : 8 * p + 8] for p in range(PER)]
    edge_columns = jnp.transpose(e.haux[i])[120:128, :]
    at_start = (first + (i == 0).astype(jnp.int32)) == 2
    e.ds[0:8, :] = jnp.where(at_start, -1.0, edge_columns)
    for p in range(PER):
        e.tile[PER * i + p] = tiles[p]
        e.ds[8 + p * L : 8 + (p + 1) * L, :] = jnp.transpose(tiles[p])
    e.col[i] = e.ds[...]
    doc = e.ds[8:, 4:5]
    summed = taps[3:4, :] * e.xs[8:, :]
    for o in (1, 2, 3):
        same = e.ds[8 - o : 8 - o + ROWS, 4:5] == doc
        summed = summed + taps[3 - o : 4 - o, :] * jnp.where(
            same, e.xs[8 - o : 8 - o + ROWS, :], 0.0
        )
    e.summed[pl.ds(r0, ROWS), :] = summed
    active = summed / (1.0 + jnp.exp(-summed))
    q = active[:, :DK]
    k = active[:, DK : 2 * DK]
    q = q * lax.rsqrt(jnp.sum(q * q, -1, keepdims=True) + EPS) * DK**-0.5
    k = k * lax.rsqrt(jnp.sum(k * k, -1, keepdims=True) + EPS)
    e.q[pl.ds(r0, ROWS), :] = q
    e.k[pl.ds(r0, ROWS), :] = k

    chains = []
    for p in range(PER):
        lo = slice(p * L, (p + 1) * L)
        kp, qp = k[lo], q[lo]
        ks = split(kp)
        both = mm(stack(ks, split(qp)), ks, NT)
        inner, score = both[:L], both[L:]
        columns = e.ds[8 + p * L : 8 + (p + 1) * L, :]
        doc_before = e.ds[7 + p * L : 8 + p * L, 4:5]
        turned = jnp.transpose(kp)
        for h in range(2):
            fade, enter, cum, cum_row, doc_row, doc_last, cum_last = gates(
                tiles[p], h, columns[:, 4:5], doc_before, columns
            )
            rate = columns[:, 2 + h : 3 + h]
            tail_row = jnp.where(doc_row == doc_last, jnp.exp(cum_last - cum_row), 0.0)
            keep = jnp.where(doc_last == doc_before, jnp.exp(cum_last), 0.0)
            chains.append(
                dict(
                    n=(PER * i + p) * 2 + h,
                    low=jnp.where(ri > ci, rate * inner * fade, 0.0),
                    left=jnp.concatenate([score * fade, turned * tail_row], axis=0),
                    right=jnp.concatenate(
                        [(rate * enter) * kp, rate * active[lo, (2 + h) * DK : (3 + h) * DK]], axis=1
                    ),
                    eq=enter * qp,
                    keep=keep,
                )
            )
    inverse = invert([c["low"] for c in chains])
    for c, t in zip(chains, inverse):
        n = c["n"]
        ts = split(t)
        ns = split(mm(split(c["left"]), ts))
        e.nh[n] = ns[0]
        e.nl[n] = ns[1]
        big = wide(stack(ts, ns), split(c["right"]))
        ws = split(jnp.concatenate([big[:L, :DK], c["eq"] - big[L : 2 * L, :DK]], axis=0))
        e.wh[n] = ws[0]
        e.wl[n] = ws[1]
        e.u[n] = big[:L, DK:]
        e.o[n] = big[L : 2 * L, DK:]
        a = split(jnp.where(ri == ci, c["keep"], 0.0) - big[2 * L :, :DK])
        e.ah[n] = a[0]
        e.al[n] = a[1]
        e.b[n] = big[2 * L :, DK:]


def backward_terms(e, i):
    for p in range(PER):
        rb = pl.multiple_of(i * ROWS + p * L, L)
        for h in range(2):
            n = (PER * i + p) * 2 + h
            g = e.grad[pl.ds(rb, L), h * DK : (h + 1) * DK]
            turned = jnp.transpose(g.astype(f32)).astype(bf16)
            e.gt[n] = turned
            e.r[n] = mm((turned,), (e.wh[n][L:], e.wl[n][L:]))


def scan_forward(e):
    ri, ci = iotas()
    eye = jnp.where(ri == ci, 1.0, 0.0).astype(f32)
    for h in range(2):
        e.st[h] = jnp.zeros((DK, DK), f32)
        e.pi[h] = eye

    def step(i, carry):
        for h in range(2):
            n = 2 * i + h
            got = wide((e.ah[n], e.al[n]), split(jnp.concatenate([e.st[n], e.pi[n]], axis=1)))
            e.st[n + 2] = got[:, :DK] + e.b[n]
            e.pi[n + 2] = got[:, DK:]
        return carry

    lax.fori_loop(0, NB, step, 0)


def scan_backward(e):
    ri, ci = iotas()
    eye = jnp.where(ri == ci, 1.0, 0.0).astype(f32)
    for h in range(2):
        e.rt[2 * NB + h] = jnp.zeros((DK, DK), f32)
        e.ps[2 * NB + h] = eye

    def step(i, carry):
        for h in range(2):
            n = 2 * (NB - 1 - i) + h
            got = mm(split(jnp.concatenate([e.rt[n + 2], e.ps[n + 2]], axis=0)), (e.ah[n], e.al[n]))
            e.rt[n] = got[:DK] + e.r[n]
            e.ps[n] = got[DK:]
        return carry

    lax.fori_loop(0, NB, step, 0)


def last_state(e):
    for h in range(2):
        e.st[2 * NB + h] = e.st[2 * NB + h] + mm(split(e.pi[2 * NB + h]), split(e.arrived[h]))


def read_pair(e, i):
    entered = [split(e.arrived[h]) for h in range(2)]
    for p in range(PER):
        rb = pl.multiple_of(i * ROWS + p * L, L)
        for h in range(2):
            n = 2 * (PER * i + p) + h
            state = e.st[n] + mm(split(e.pi[n]), entered[h])
            e.st[n] = state
            both = mm((e.wh[n], e.wl[n]), split(state))
            e.u[n] = e.u[n] - both[:L]
            out = e.o[n] + both[L:]
            e.o[n] = out
            e.out[pl.ds(rb, L), h * DK : (h + 1) * DK] = out.astype(bf16)


def finish_pair(e, i, t, taps):
    ri, ci = iotas()
    lower = jnp.where(ri >= ci, 1.0, 0.0).astype(f32)
    r0 = pl.multiple_of(i * ROWS, ROWS)
    e.cs[0 : 8 + ROWS, :] = e.col[i]
    sm = e.summed[pl.ds(r0, ROWS), :]
    sigma = 1.0 / (1.0 + jnp.exp(-sm))
    active = sm * sigma
    left = [split(e.arrived[2 + h]) for h in range(2)]
    pieces = []
    for p in range(PER):
        lo = slice(p * L, (p + 1) * L)
        block = PER * i + p
        rb = pl.multiple_of(r0 + p * L, L)
        tile = e.tile[block]
        columns = e.cs[8 + p * L : 8 + (p + 1) * L, :]
        doc_before = e.cs[7 + p * L : 8 + p * L, 4:5]
        d_score = jnp.zeros((L, L), f32)
        d_low = jnp.zeros((L, L), f32)
        dq = jnp.zeros((L, DK), f32)
        dk = jnp.zeros((L, DK), f32)
        small = jnp.zeros((L, L), f32)
        dvs, ends = [], []
        for h in range(2):
            n = 2 * block + h
            fade, enter, cum, cum_row, doc_row, doc_last, cum_last = gates(
                tile, h, columns[:, 4:5], doc_before, columns
            )
            rate = columns[:, 2 + h : 3 + h]
            tail = jnp.where(columns[:, 4:5] == doc_last, jnp.exp(cum_last - cum), 0.0)
            state = split(e.st[n])
            later = e.rt[n + 2] + mm(left[h], split(e.ps[n + 2]))
            laters = split(later)
            u = e.u[n]
            out = e.o[n]
            g = e.grad[pl.ds(rb, L), h * DK : (h + 1) * DK]
            ns = (e.nh[n], e.nl[n])
            yt = mm((e.gt[n],), (ns[0][:L], ns[1][:L])) + mm(laters, (ns[0][L:], ns[1][L:]))
            y = jnp.transpose(yt)
            ys = split(y)
            us = split(u)
            right = stack(us, state)
            tops = jnp.concatenate([g, ys[0], ys[1]], axis=0)

            def dot(a, b):
                return lax.dot_general(a, b, NT, preferred_element_type=f32)

            res = dot(tops, right[0])
            fine = dot(tops[: 2 * L], right[1])
            gu = res[:L] + fine[:L]
            yu = res[L : 2 * L] + res[2 * L :] + fine[L:]
            d_score = d_score + gu[:, :L] * fade
            d_low = d_low - jnp.where(ri > ci, yu[:, :L] * (rate * fade), 0.0)
            dq = dq + enter * gu[:, L:]
            dk = dk - (enter * rate) * yu[:, L:]
            dv = rate * y
            dvs.append(dv)
            ends.append((us, tail, laters))
            v = active[lo, (2 + h) * DK : (3 + h) * DK]
            d_cum = jnp.sum(out * g.astype(f32) - v * dv, -1, keepdims=True)
            end = jnp.sum(e.st[n + 2] * jnp.transpose(later), -1, keepdims=True)
            end = jnp.sum(end, 0, keepdims=True)
            d_cum = d_cum + jnp.where(ri[:, 0:1] == L - 1, end, 0.0)
            d_rate = jnp.sum(y * u, -1, keepdims=True) / rate
            small = small + jnp.where(ci == h, d_cum, 0.0) + jnp.where(ci == 2 + h, d_rate, 0.0)
        ks = split(e.k[pl.ds(rb, L), :])
        qs = split(e.q[pl.ds(rb, L), :])
        both = mm(split(jnp.concatenate([d_score, d_low + jnp.transpose(d_low)], axis=0)), ks)
        dq = dq + both[:L]
        dk = dk + both[L:] + mm(split(jnp.transpose(d_score)), qs)
        for us, tail, laters in ends:
            dk = dk + tail * mm(us, laters)
        small = jnp.transpose(small)[0:8, :]
        which = lax.broadcasted_iota(jnp.int32, (8, 128), 0)
        e.daux[block] = jnp.where(which < 2, exact(small, lower), small)
        pieces.append((dq, dk, dvs[0], dvs[1]))
    dq, dk, dv0, dv1 = (jnp.concatenate(x, axis=0) for x in zip(*pieces))
    aq, ak = active[:, :DK], active[:, DK : 2 * DK]
    nq = lax.rsqrt(jnp.sum(aq * aq, -1, keepdims=True) + EPS)
    nk = lax.rsqrt(jnp.sum(ak * ak, -1, keepdims=True) + EPS)
    dq = dq * DK**-0.5
    dq = nq * (dq - aq * (nq * nq * jnp.sum(aq * dq, -1, keepdims=True)))
    dk = nk * (dk - ak * (nk * nk * jnp.sum(ak * dk, -1, keepdims=True)))
    d_all = jnp.concatenate([dq, dk, dv0, dv1], axis=1)
    d_sum = d_all * (sigma * (1.0 + sm * (1.0 - sigma)))
    e.gs[8 : 8 + ROWS, :] = d_sum

    x = e.rows[pl.ds(r0, ROWS), :].astype(f32)
    doc = e.cs[8 : 8 + ROWS, 4:5]
    before = e.cs[0:8, 4:5]
    xh = e.halo[i][8:16, :].astype(f32)
    dx = taps[3:4, :] * d_sum
    back = jnp.zeros((8, 4 * DK), f32)
    parts = [jnp.sum(d_sum * x, 0, keepdims=True)]
    for o in (1, 2, 3):
        tap = taps[3 - o : 4 - o, :]
        moved = jnp.where(
            e.cs[8 + o : 8 + o + ROWS, 4:5] == doc, e.gs[8 + o : 8 + o + ROWS, :], 0.0
        )
        dx = dx + tap * moved
        over = jnp.where(e.cs[o : o + 8, 4:5] == before, e.gs[o : o + 8, :], 0.0)
        back = back + tap * over
        parts.append(
            jnp.sum(moved * x, 0, keepdims=True) + jnp.sum(over * xh, 0, keepdims=True)
        )
    rest = jnp.where((t > 0) & (i < CHIPS - 1), e.back[lax.rem(t + 3, CHIPS)], 0.0)
    edge = dx[ROWS - 8 :, :] + rest
    e.dmix[pl.ds(r0, ROWS), :] = jnp.concatenate([dx[: ROWS - 8, :], edge], axis=0).astype(bf16)
    e.edge[t] = edge
    e.back[t] = back
    e.taps[...] = e.taps[...] + jnp.concatenate(parts[::-1], axis=0)


def start_finish(e):
    e.gs[0:8, :] = jnp.zeros((8, 4 * DK), f32)
    e.gs[8 + ROWS :, :] = jnp.zeros((8, 4 * DK), f32)
    e.cs[8 + ROWS :, :] = jnp.full((8, 8), -2.0, f32)
    e.taps[...] = jnp.zeros((4, 4 * DK), f32)
    e.back[...] = jnp.zeros((CHIPS, 8, 4 * DK), f32)


def head_taps(weight, j):
    wq = weight[:, pl.ds(pl.multiple_of(j * DK, DK), DK)]
    wk = weight[:, pl.ds(pl.multiple_of((KH + j) * DK, DK), DK)]
    wv = weight[:, pl.ds(pl.multiple_of((2 * KH + 2 * j) * DK, 2 * DK), 2 * DK)]
    return jnp.concatenate([wq.astype(f32), wk.astype(f32), wv.astype(f32)], axis=1)


SQ = (2 * NB, DK, DK)
SCRATCH = dict(
    rows=((QUARTER, 4 * DK), bf16),
    grad=((QUARTER, 2 * DK), bf16),
    aux=((GROUP, 8, 128), f32),
    halo=((CHIPS, 16, 4 * DK), bf16),
    haux=((CHIPS, 8, 128), f32),
    xs=((8 + ROWS, 4 * DK), f32),
    ds=((8 + ROWS, 8), f32),
    tile=((NB, 8, 128), f32),
    col=((CHIPS, 8 + ROWS, 8), f32),
    summed=((QUARTER, 4 * DK), f32),
    q=((QUARTER, DK), f32),
    k=((QUARTER, DK), f32),
    nh=((2 * NB, 2 * L, L), bf16),
    nl=((2 * NB, 2 * L, L), bf16),
    wh=((2 * NB, 2 * L, DK), bf16),
    wl=((2 * NB, 2 * L, DK), bf16),
    ah=(SQ, bf16),
    al=(SQ, bf16),
    u=(SQ, f32),
    o=(SQ, f32),
    b=(SQ, f32),
    r=(SQ, f32),
    gt=(SQ, bf16),
    st=((2 * NB + 2, DK, DK), f32),
    rt=((2 * NB + 2, DK, DK), f32),
    pi=((2 * NB + 2, DK, DK), f32),
    ps=((2 * NB + 2, DK, DK), f32),
    arrived=((4, DK, DK), f32),
    cs=((16 + ROWS, 8), f32),
    gs=((16 + ROWS, 4 * DK), f32),
    out=((QUARTER, 2 * DK), bf16),
    dmix=((QUARTER, 4 * DK), bf16),
    edge=((CHIPS, 8, 4 * DK), f32),
    back=((CHIPS, 8, 4 * DK), f32),
    taps=((4, 4 * DK), f32),
    daux=((GROUP, 8, 128), f32),
)


ARGS = ("mixed", "weight", "decay", "rate", "docs", "grad_in")
OUTS = ("o_out", "o_mix", "o_taps", "o_decay", "o_rate")
EXTRA = dict(
    aux_own=((GROUP, 8, 128), f32),
    edges=((GROUP, 8, 4 * DK), f32),
    backs=((GROUP, 8, 4 * DK), f32),
    part=((16, 4, 4 * DK), f32),
    total=((4, 4 * DK), f32),
    gathered=((GROUP, 4, 4 * DK), f32),
    daux_in=((GROUP, 8, 128), f32),
)
SEMS = dict(
    asend=(GROUP, 5),
    arecv=(GROUP, 5),
    hsend=(GROUP, 4),
    hrecv=(CHIPS, 4),
    ssend=(2,),
    srecv=(2,),
    bsend=(CHIPS,),
    brecv=(GROUP,),
    esend=(CHIPS,),
    erecv=(GROUP,),
    fsend=(GROUP, 5),
    frecv=(GROUP, 5),
    tsend=(16,),
    trecv=(16,),
    gsend=(GROUP,),
    grecv=(GROUP,),
)
NAMES = ARGS + OUTS + tuple(SCRATCH) + tuple(EXTRA) + tuple(SEMS)


def head_columns(to):
    return (
        pl.ds(pl.multiple_of(to * DK, DK), DK),
        pl.ds(pl.multiple_of((KH + to) * DK, DK), DK),
        pl.ds(pl.multiple_of((2 * KH + 2 * to) * DK, 2 * DK), 2 * DK),
    )


OWN = (pl.ds(0, DK), pl.ds(DK, DK), pl.ds(2 * DK, 2 * DK))


def two_columns(to):
    return pl.ds(pl.multiple_of(to * 2 * DK, 2 * DK), 2 * DK)


def place(j):
    return pl.ds(pl.multiple_of(j * 128, 128), 128)


def layer_kernel(*refs):
    e = types.SimpleNamespace(**dict(zip(NAMES, refs)))
    dp = lax.axis_index("dp")
    me = lax.axis_index("seq")
    row, j = me // GROUP, lax.rem(me, GROUP)
    y, c = j // 2, lax.rem(j, 2)
    base = row * GROUP
    last = GROUP - 1
    before = lax.rem(row + 3, 4) * GROUP
    after = lax.rem(row + 1, 4) * GROUP
    is_last = j == last
    first = (row == 0).astype(jnp.int32)

    def remote(src, dst, send, recv, seq, slab=None):
        return pltpu.make_async_remote_copy(
            src_ref=src,
            dst_ref=dst,
            send_sem=send,
            recv_sem=recv,
            device_id=(dp if slab is None else slab, seq),
            device_id_type=MESH,
        )

    def peer(dy, dc):
        return 2 * lax.rem(y + dy, CHIPS) + lax.rem(c + dc, 2)

    def plane(n):
        return lax.rem(dp + n // 4, 4), lax.rem(me + (n % 4) * GROUP, 4 * GROUP)

    barrier = pltpu.get_barrier_semaphore()

    def greet(slab, seq):
        pl.semaphore_signal(barrier, inc=1, device_id=(slab, seq), device_id_type=MESH)

    for s in range(1, GROUP):
        greet(dp, base + lax.rem(j + s, GROUP))
    for n in range(1, 16):
        greet(*plane(n))
    greet(dp, before + last)

    @pl.when(is_last)
    def _():
        for to in range(GROUP):
            greet(dp, after + to)

    docs = e.docs[...].astype(f32)
    for to in range(GROUP):
        e.aux_own[to] = jnp.concatenate(
            [
                e.decay[2 * to : 2 * to + 2, :],
                e.rate[2 * to : 2 * to + 2, :],
                docs,
                jnp.zeros((3, 128), f32),
            ],
            axis=0,
        )
    taps = head_taps(e.weight, j)
    pl.semaphore_wait(barrier, jnp.where(is_last, GROUP - 1 + 15 + 1 + GROUP, GROUP - 1 + 15 + 1))

    slot = lax.rem(y + 1, CHIPS)
    inside = y < CHIPS - 1
    there = jnp.where(inside, base, after)

    def halo_copies(to, at, group):
        own = head_columns(to)
        r = pl.ds(112, 16)
        pairs = [(e.mixed.at[r, own[n]], e.halo.at[at, :, OWN[n]]) for n in range(3)]
        pairs.append((e.aux_own.at[to], e.haux.at[at]))
        return [
            remote(src, dst, e.hsend.at[to, n], e.hrecv.at[at, n], group + to)
            for n, (src, dst) in enumerate(pairs)
        ]

    @pl.when(c == 1)
    def _():
        for to in range(GROUP):

            @pl.when(jnp.logical_not(inside) | (j != to))
            def _():
                for copy in halo_copies(to, slot, there):
                    copy.start()

        @pl.when(inside)
        def _():
            own = head_columns(j)
            for n in range(3):
                e.halo[slot, :, OWN[n]] = e.mixed[112:128, own[n]]
            e.haux[slot] = e.aux_own[j]

    def dy_of(t):
        return t + t // 2 - 2 * (t // 3)

    def head_copy(t, dc, n):
        to = peer(dy_of(t), dc)
        own = head_columns(to)
        at = place(j)
        src, dst = (
            (e.mixed.at[:, own[0]], e.rows.at[at, OWN[0]]),
            (e.mixed.at[:, own[1]], e.rows.at[at, OWN[1]]),
            (e.mixed.at[:, own[2]], e.rows.at[at, OWN[2]]),
            (e.aux_own.at[to], e.aux.at[j]),
            (e.grad_in.at[:, two_columns(to)], e.grad.at[at, :]),
        )[n]
        k = 2 * t + dc
        return remote(src, dst, e.asend.at[k, n], e.arecv.at[k, n], base + to)

    steps = [(t, dc) for t in range(CHIPS) for dc in range(2) if (t, dc) != (0, 0)]
    for t, dc in steps:
        for n in range(4):
            head_copy(t, dc, n).start()
    for t, dc in steps:
        head_copy(t, dc, 4).start()

    own = head_columns(j)
    for n in range(3):
        e.rows[place(j), OWN[n]] = e.mixed[:, own[n]]
    e.aux[j] = e.aux_own[j]
    e.grad[place(j), :] = e.grad_in[:, two_columns(j)]

    def pair_of(t):
        return lax.rem(y + CHIPS - dy_of(t), CHIPS)

    def prepare(t, carry):
        i = pair_of(t)

        @pl.when(t > 0)
        def _():
            for n in range(4):
                head_copy(t, 0, n).wait_recv()

        for n in range(4):
            head_copy(t, 1, n).wait_recv()

        @pl.when((i == 0) | (2 * i - 1 != j))
        def _():
            for copy in halo_copies(0, i, base):
                copy.wait_recv()

        prepare_pair(e, i, first, taps)
        return carry

    lax.fori_loop(0, CHIPS, prepare, 0)

    def hop(n, src, to):
        return remote(src, e.arrived.at[pl.ds(2 * n, 2)], e.ssend.at[n], e.srecv.at[n], to)

    forth = hop(0, e.st.at[pl.ds(2 * NB, 2)], lax.rem(me + GROUP, 4 * GROUP))
    back = hop(1, e.rt.at[pl.ds(0, 2)], lax.rem(me + 3 * GROUP, 4 * GROUP))
    scan_forward(e)
    start_finish(e)
    forth.start()

    def turn(t, carry):
        @pl.when(t > 0)
        def _():
            head_copy(t, 0, 4).wait_recv()

        head_copy(t, 1, 4).wait_recv()
        backward_terms(e, pair_of(t))
        return carry

    lax.fori_loop(0, CHIPS, turn, 0)
    scan_backward(e)
    for t, dc in steps:
        for n in range(5):
            head_copy(t, dc, n).wait_send()

    @pl.when(c == 1)
    def _():
        for to in range(GROUP):

            @pl.when(jnp.logical_not(inside) | (j != to))
            def _():
                for copy in halo_copies(to, slot, there):
                    copy.wait_send()

    back.start()
    forth.wait()
    last_state(e)

    def token_copy(t, dc, n):
        to = peer(CHIPS - 1 - t, dc)
        r = place(to)
        own = head_columns(j)
        src, dst = (
            (e.out.at[r, :], e.o_out.at[:, two_columns(j)]),
            (e.dmix.at[r, OWN[0]], e.o_mix.at[:, own[0]]),
            (e.dmix.at[r, OWN[1]], e.o_mix.at[:, own[1]]),
            (e.dmix.at[r, OWN[2]], e.o_mix.at[:, own[2]]),
            (e.daux.at[to], e.daux_in.at[j]),
        )[n]
        k = 2 * t + dc
        return remote(src, dst, e.fsend.at[k, n], e.frecv.at[k, n], base + to)

    def target(t):
        return lax.rem(y + CHIPS - 1 - t, CHIPS)

    def read(t, carry):
        read_pair(e, target(t))

        @pl.when(t < CHIPS - 1)
        def _():
            token_copy(t, 0, 0).start()

        token_copy(t, 1, 0).start()
        return carry

    lax.fori_loop(0, CHIPS, read, 0)
    back.wait()

    def edge_copy(i, at):
        return remote(
            e.edge.at[at], e.edges.at[j], e.esend.at[at], e.erecv.at[j], base + 2 * i + 1
        )

    def edge_goes(i, t):
        return ((i == CHIPS - 1) & (j != last)) | ((t == 0) & (i < CHIPS - 1))

    def back_copy(i, at):
        to = jnp.where(i == 0, before + last, base + 2 * i - 1)
        return remote(e.back.at[at], e.backs.at[j], e.bsend.at[at], e.brecv.at[j], to)

    def back_goes(i, t):
        return (i == 0) | (t == CHIPS - 1)

    def finish(t, carry):
        i = target(t)
        finish_pair(e, i, t, taps)

        @pl.when(t < CHIPS - 1)
        def _():
            for n in range(1, 5):
                token_copy(t, 0, n).start()

        for n in range(1, 5):
            token_copy(t, 1, n).start()

        @pl.when(edge_goes(i, t))
        def _():
            edge_copy(i, t).start()

        @pl.when((i == CHIPS - 1) & (j == last))
        def _():
            e.edges[j] = e.edge[t]

        @pl.when(back_goes(i, t))
        def _():
            back_copy(i, t).start()

        return carry

    lax.fori_loop(0, CHIPS, finish, 0)

    spot = 4 * dp + row

    def tap_copy(n):
        slab, seq = plane(n)
        return remote(e.taps.at[:, :], e.part.at[spot], e.tsend.at[n], e.trecv.at[n], seq, slab)

    for n in range(1, 16):
        tap_copy(n).start()

    own = head_columns(j)
    e.o_out[:, two_columns(j)] = e.out[place(j), :]
    for n in range(3):
        e.o_mix[:, own[n]] = e.dmix[place(j), OWN[n]]
    e.daux_in[j] = e.daux[j]

    for n in range(1, 16):
        tap_copy(n).wait_recv()
    e.part[spot] = e.taps[...]
    whole = e.part[0]
    for n in range(1, 16):
        whole = whole + e.part[n]
    e.total[...] = whole
    e.gathered[j] = whole

    def gather_copy(s):
        return remote(
            e.total.at[:, :],
            e.gathered.at[j],
            e.gsend.at[s],
            e.grecv.at[s],
            base + lax.rem(j + s, GROUP),
        )

    for s in range(1, GROUP):
        gather_copy(s).start()

    for t in range(CHIPS):
        for dc in range(2):
            if (t, dc) != (CHIPS - 1, 0):
                for n in range(5):
                    token_copy(t, dc, n).wait()

    @pl.when(c == 1)
    def _():
        for src in range(GROUP):

            def edge_from():
                return remote(
                    e.edge.at[0], e.edges.at[src], e.esend.at[0], e.erecv.at[src], base + last
                )

            def back_from():
                return remote(
                    e.back.at[0], e.backs.at[src], e.bsend.at[0], e.brecv.at[src], base + last
                )

            whole_row = y == CHIPS - 1

            @pl.when(whole_row | (y + 1 == src // 2))
            def _():
                @pl.when(j != src)
                def _():
                    edge_from().wait_recv()

                back_from().wait_recv()
                fixed = e.edges[src] + e.backs[src]
                spots = (
                    (src * DK, DK, 0),
                    ((KH + src) * DK, DK, DK),
                    ((2 * KH + 2 * src) * DK, 2 * DK, 2 * DK),
                )
                for at, width, own_at in spots:
                    old = e.o_mix[112:128, at : at + width].astype(f32)
                    new = jnp.concatenate([old[0:8], fixed[:, own_at : own_at + width]], axis=0)
                    e.o_mix[112:128, at : at + width] = new.astype(bf16)

    for src in range(GROUP):
        e.o_decay[2 * src : 2 * src + 2, :] = e.daux_in[src][0:2, :]
        e.o_rate[2 * src : 2 * src + 2, :] = e.daux_in[src][2:4, :]

    for s in range(1, GROUP):
        gather_copy(s).wait()
    for src in range(GROUP):
        got = e.gathered[src]
        e.o_taps[:, src * DK : (src + 1) * DK] = got[:, 0:DK]
        e.o_taps[:, (KH + src) * DK : (KH + src + 1) * DK] = got[:, DK : 2 * DK]
        e.o_taps[:, (2 * KH + 2 * src) * DK : (2 * KH + 2 * src + 2) * DK] = got[:, 2 * DK :]

    for n in range(1, 16):
        tap_copy(n).wait_send()
    for t in range(CHIPS):
        i = target(t)

        @pl.when(edge_goes(i, t))
        def _():
            edge_copy(i, t).wait_send()

        @pl.when(back_goes(i, t))
        def _():
            back_copy(i, t).wait_send()


def layer(*args):
    scratch = [VM(*x) for x in SCRATCH.values()] + [VM(*x) for x in EXTRA.values()]
    return pl.pallas_call(
        layer_kernel,
        out_shape=(
            jax.ShapeDtypeStruct((128, 2 * KH * DK), bf16),
            jax.ShapeDtypeStruct((128, 4 * KH * DK), bf16),
            jax.ShapeDtypeStruct((4, 4 * KH * DK), f32),
            jax.ShapeDtypeStruct((VH, 128), f32),
            jax.ShapeDtypeStruct((VH, 128), f32),
        ),
        in_specs=[vspec] * len(ARGS),
        out_specs=(vspec,) * len(OUTS),
        scratch_shapes=scratch + [pltpu.SemaphoreType.DMA(x) for x in SEMS.values()],
        compiler_params=pltpu.CompilerParams(
            collective_id=0, has_side_effects=True, vmem_limit_bytes=60 * 1024 * 1024
        ),
        name="layer",
    )(*args)


def emit_kernel(*refs):
    for src, dst in zip(refs[:5], refs[5:]):
        dst[...] = src[...]


def emit(*arrays):
    return pl.pallas_call(
        emit_kernel,
        out_shape=tuple(jax.ShapeDtypeStruct(x.shape, x.dtype) for x in arrays),
        in_specs=[vspec] * 5,
        out_specs=(vspec,) * 5,
        name="emit",
    )(*arrays)


def local(mixed, conv_weight, log_decay, beta, doc_ids, out_grad):
    out, dmix, taps, d_decay, d_beta = layer(
        mixed[0], conv_weight, log_decay[0], beta[0], doc_ids, out_grad[0]
    )
    out, dmix, taps, d_decay, d_beta = emit(out, dmix, taps, d_decay, d_beta)
    return out[None], dmix[None], taps, d_decay[None], d_beta[None]


def solution(mesh):
    in_specs = (
        P("dp", "seq", None),
        P(),
        P("dp", None, "seq"),
        P("dp", None, "seq"),
        P("dp", "seq"),
        P("dp", "seq", None),
    )
    out_specs = (
        P("dp", "seq", None),
        P("dp", "seq", None),
        P(),
        P("dp", None, "seq"),
        P("dp", None, "seq"),
    )
    return jax.shard_map(local, mesh=mesh, in_specs=in_specs, out_specs=out_specs, check_vma=False)
```

```python
import types

import jax
import jax.numpy as jnp
from jax import lax
from jax.experimental import pallas as pl
from jax.experimental.pallas import tpu as pltpu
from jax.sharding import PartitionSpec as P

DK = 128
KH = 8
VH = 16
L = 128
GROUP = 8
CHIPS = GROUP // 2
QUARTER = GROUP * 128
NB = QUARTER // L
PER = 2
ROWS = PER * L
EPS = 1e-6

f32 = jnp.float32
bf16 = jnp.bfloat16
NN = (((1,), (0,)), ((), ()))
NT = (((1,), (1,)), ((), ()))
MESH = pl.DeviceIdType.MESH
VM = pltpu.VMEM
vspec = pl.BlockSpec(memory_space=pltpu.VMEM)


def split(a):
    high = a.astype(bf16)
    return high, (a - high.astype(f32)).astype(bf16)


def stack(*pairs):
    return tuple(jnp.concatenate(x, axis=0) for x in zip(*pairs))


def mm(a, b, dims=NN):
    def dot(p, q):
        return lax.dot_general(p, q, dims, preferred_element_type=f32)

    if len(a) == 1:
        return dot(a[0], b[0]) + dot(a[0], b[1])
    rows = a[0].shape[0]
    both = dot(jnp.concatenate(a, axis=0), b[0])
    return both[:rows] + both[rows:] + dot(a[0], b[1])


def wide(a, b):
    left = jnp.concatenate([a[0], a[1], a[0]], axis=1)
    right = jnp.concatenate([b[0], b[0], b[1]], axis=0)
    return lax.dot_general(left, right, NN, preferred_element_type=f32)


def exact(a, b):
    return lax.dot_general(a, b, NN, preferred_element_type=f32, precision=lax.Precision.HIGHEST)


def iotas(rows=L):
    return (
        lax.broadcasted_iota(jnp.int32, (rows, L), 0),
        lax.broadcasted_iota(jnp.int32, (rows, L), 1),
    )


def invert(lows):
    ri, ci = iotas()
    eye = jnp.where(ri == ci, 1.0, 0.0).astype(f32)
    near = ri // 8 == ci // 8
    d = [jnp.where(near, x, 0.0) for x in lows]
    s1 = [split(x) for x in d]
    d2 = [mm(x, x) for x in s1]
    s2 = [split(x) for x in d2]
    d34 = [mm(stack(x, y), y) for x, y in zip(s1, s2)]
    inverse = [eye - x + y - z[:L] for x, y, z in zip(d, d2, d34)]
    inverse = [x + mm(split(x), split(z[L:])) for x, z in zip(inverse, d34)]
    half, lane = iotas(L // 2)
    size = 8
    while size < L:
        spots = range(0, L, 2 * size)
        mask = lane // size == 2 * (half // size)
        corner = [
            jnp.where(mask, jnp.concatenate([x[r + size : r + 2 * size] for r in spots], 0), 0.0)
            for x in lows
        ]
        inner = [mm(split(c), split(x)) for c, x in zip(corner, inverse)]
        zero = jnp.zeros((size, L), f32)
        spread = [
            jnp.concatenate(
                [p for m in range(len(spots)) for p in (zero, y[m * size : (m + 1) * size])], 0
            )
            for y in inner
        ]
        odd = [jnp.concatenate([x[r + size : r + 2 * size] for r in spots], 0) for x in inverse]
        odd = [x - mm(split(x), split(y)) for x, y in zip(odd, spread)]
        inverse = [
            jnp.concatenate(
                [
                    p
                    for m, r in enumerate(spots)
                    for p in (x[r : r + size], o[m * size : (m + 1) * size])
                ],
                0,
            )
            for x, o in zip(inverse, odd)
        ]
        size *= 2
    return inverse


def gates(tile, h, doc_column, doc_before, columns):
    ri, ci = iotas()
    doc_row = tile[4:5, :]
    cum = columns[:, h : h + 1]
    cum_row = tile[h : h + 1, :]
    doc_last = tile[4:5, L - 1 : L]
    cum_last = tile[h : h + 1, L - 1 : L]
    fade = jnp.where(
        (doc_column == doc_row) & (ri >= ci), jnp.exp(jnp.minimum(cum - cum_row, 0.0)), 0.0
    )
    enter = jnp.where(doc_column == doc_before, jnp.exp(cum), 0.0)
    return fade, enter, cum, cum_row, doc_row, doc_last, cum_last


def prepare_pair(e, i, first, taps):
    ri, ci = iotas()
    r0 = pl.multiple_of(i * ROWS, ROWS)
    e.xs[0:8, :] = e.halo[i][8:16, :].astype(f32)
    e.xs[8:, :] = e.rows[pl.ds(r0, ROWS), :].astype(f32)
    upper = jnp.where(ri <= ci, 1.0, 0.0).astype(f32)
    flat = jnp.concatenate([e.aux[PER * i + p] for p in range(PER)], axis=0)
    sums = exact(flat, upper)
    which = lax.rem(lax.broadcasted_iota(jnp.int32, (PER * 8, 128), 0), 8)
    flat = jnp.where(which < 2, sums, flat)
    tiles = [flat[8 * p : 8 * p + 8] for p in range(PER)]
    edge_columns = jnp.transpose(e.haux[i])[120:128, :]
    at_start = (first + (i == 0).astype(jnp.int32)) == 2
    e.ds[0:8, :] = jnp.where(at_start, -1.0, edge_columns)
    for p in range(PER):
        e.tile[PER * i + p] = tiles[p]
        e.ds[8 + p * L : 8 + (p + 1) * L, :] = jnp.transpose(tiles[p])
    e.col[i] = e.ds[...]
    doc = e.ds[8:, 4:5]
    summed = taps[3:4, :] * e.xs[8:, :]
    for o in (1, 2, 3):
        same = e.ds[8 - o : 8 - o + ROWS, 4:5] == doc
        summed = summed + taps[3 - o : 4 - o, :] * jnp.where(
            same, e.xs[8 - o : 8 - o + ROWS, :], 0.0
        )
    e.summed[pl.ds(r0, ROWS), :] = summed
    active = summed / (1.0 + jnp.exp(-summed))
    q = active[:, :DK]
    k = active[:, DK : 2 * DK]
    q = q * lax.rsqrt(jnp.sum(q * q, -1, keepdims=True) + EPS) * DK**-0.5
    k = k * lax.rsqrt(jnp.sum(k * k, -1, keepdims=True) + EPS)
    e.q[pl.ds(r0, ROWS), :] = q
    e.k[pl.ds(r0, ROWS), :] = k

    chains = []
    for p in range(PER):
        lo = slice(p * L, (p + 1) * L)
        kp, qp = k[lo], q[lo]
        ks = split(kp)
        both = mm(stack(ks, split(qp)), ks, NT)
        inner, score = both[:L], both[L:]
        columns = e.ds[8 + p * L : 8 + (p + 1) * L, :]
        doc_before = e.ds[7 + p * L : 8 + p * L, 4:5]
        turned = jnp.transpose(kp)
        for h in range(2):
            fade, enter, cum, cum_row, doc_row, doc_last, cum_last = gates(
                tiles[p], h, columns[:, 4:5], doc_before, columns
            )
            rate = columns[:, 2 + h : 3 + h]
            tail_row = jnp.where(doc_row == doc_last, jnp.exp(cum_last - cum_row), 0.0)
            keep = jnp.where(doc_last == doc_before, jnp.exp(cum_last), 0.0)
            chains.append(
                dict(
                    n=(PER * i + p) * 2 + h,
                    low=jnp.where(ri > ci, rate * inner * fade, 0.0),
                    left=jnp.concatenate([score * fade, turned * tail_row], axis=0),
                    right=jnp.concatenate(
                        [(rate * enter) * kp, rate * active[lo, (2 + h) * DK : (3 + h) * DK]], axis=1
                    ),
                    eq=enter * qp,
                    keep=keep,
                )
            )
    inverse = [split(t) for t in invert([c["low"] for c in chains])]
    lefts = [split(mm(split(c["left"]), t)) for c, t in zip(chains, inverse)]
    bigs = [wide(stack(t, x), split(c["right"])) for c, t, x in zip(chains, inverse, lefts)]
    for c, ns, big in zip(chains, lefts, bigs):
        n = c["n"]
        e.nh[n] = ns[0]
        e.nl[n] = ns[1]
        ws = split(jnp.concatenate([big[:L, :DK], c["eq"] - big[L : 2 * L, :DK]], axis=0))
        e.wh[n] = ws[0]
        e.wl[n] = ws[1]
        e.u[n] = big[:L, DK:]
        e.o[n] = big[L : 2 * L, DK:]
        a = split(jnp.where(ri == ci, c["keep"], 0.0) - big[2 * L :, :DK])
        e.ah[n] = a[0]
        e.al[n] = a[1]
        e.b[n] = big[2 * L :, DK:]


def backward_terms(e, i):
    for p in range(PER):
        rb = pl.multiple_of(i * ROWS + p * L, L)
        for h in range(2):
            n = (PER * i + p) * 2 + h
            g = e.grad[pl.ds(rb, L), h * DK : (h + 1) * DK]
            turned = jnp.transpose(g.astype(f32)).astype(bf16)
            e.gt[n] = turned
            e.r[n] = mm((turned,), (e.wh[n][L:], e.wl[n][L:]))


def scan_forward(e):
    ri, ci = iotas()
    eye = jnp.where(ri == ci, 1.0, 0.0).astype(f32)
    for h in range(2):
        e.st[h] = jnp.zeros((DK, DK), f32)
        e.pi[h] = eye

    def step(i, carry):
        for h in range(2):
            n = 2 * i + h
            got = wide((e.ah[n], e.al[n]), split(jnp.concatenate([e.st[n], e.pi[n]], axis=1)))
            e.st[n + 2] = got[:, :DK] + e.b[n]
            e.pi[n + 2] = got[:, DK:]
        return carry

    lax.fori_loop(0, NB, step, 0)


def scan_backward(e):
    ri, ci = iotas()
    eye = jnp.where(ri == ci, 1.0, 0.0).astype(f32)
    for h in range(2):
        e.rt[2 * NB + h] = jnp.zeros((DK, DK), f32)
        e.ps[2 * NB + h] = eye

    def step(i, carry):
        for h in range(2):
            n = 2 * (NB - 1 - i) + h
            got = mm(split(jnp.concatenate([e.rt[n + 2], e.ps[n + 2]], axis=0)), (e.ah[n], e.al[n]))
            e.rt[n] = got[:DK] + e.r[n]
            e.ps[n] = got[DK:]
        return carry

    lax.fori_loop(0, NB, step, 0)


def last_state(e):
    for h in range(2):
        e.st[2 * NB + h] = e.st[2 * NB + h] + mm(split(e.pi[2 * NB + h]), split(e.arrived[h]))


def read_pair(e, i):
    entered = [split(e.arrived[h]) for h in range(2)]
    for p in range(PER):
        rb = pl.multiple_of(i * ROWS + p * L, L)
        for h in range(2):
            n = 2 * (PER * i + p) + h
            state = e.st[n] + mm(split(e.pi[n]), entered[h])
            e.st[n] = state
            both = mm((e.wh[n], e.wl[n]), split(state))
            e.u[n] = e.u[n] - both[:L]
            out = e.o[n] + both[L:]
            e.o[n] = out
            e.out[pl.ds(rb, L), h * DK : (h + 1) * DK] = out.astype(bf16)


def finish_pair(e, i, t, taps):
    ri, ci = iotas()
    lower = jnp.where(ri >= ci, 1.0, 0.0).astype(f32)
    r0 = pl.multiple_of(i * ROWS, ROWS)
    e.cs[0 : 8 + ROWS, :] = e.col[i]
    sm = e.summed[pl.ds(r0, ROWS), :]
    sigma = 1.0 / (1.0 + jnp.exp(-sm))
    active = sm * sigma
    left = [split(e.arrived[2 + h]) for h in range(2)]

    def dot(a, b):
        return lax.dot_general(a, b, NT, preferred_element_type=f32)

    spots = [(p, h) for p in range(PER) for h in range(2)]
    index = [2 * (PER * i + p) + h for p, h in spots]
    starts = [pl.multiple_of(r0 + p * L, L) for p in range(PER)]
    later = [
        e.rt[n + 2] + mm(left[h], split(e.ps[n + 2])) for (p, h), n in zip(spots, index)
    ]
    laters = [split(x) for x in later]
    turned = [
        mm((e.gt[n],), (e.nh[n][:L], e.nl[n][:L])) + mm(x, (e.nh[n][L:], e.nl[n][L:]))
        for n, x in zip(index, laters)
    ]
    ys = [jnp.transpose(x) for x in turned]
    us = [split(e.u[n]) for n in index]
    states = [split(e.st[n]) for n in index]
    grads = [e.grad[pl.ds(starts[p], L), h * DK : (h + 1) * DK] for p, h in spots]
    tops = [jnp.concatenate((g,) + split(y), axis=0) for g, y in zip(grads, ys)]
    rights = [stack(u, x) for u, x in zip(us, states)]
    res = [dot(a, b[0]) for a, b in zip(tops, rights)]
    fine = [dot(a[: 2 * L], b[1]) for a, b in zip(tops, rights)]
    tails = [mm(u, x) for u, x in zip(us, laters)]
    pieces, scores, lows = [], [], []
    for p in range(PER):
        block = PER * i + p
        rb = starts[p]
        tile = e.tile[block]
        columns = e.cs[8 + p * L : 8 + (p + 1) * L, :]
        doc_before = e.cs[7 + p * L : 8 + p * L, 4:5]
        d_score = d_low = dq = dk = 0.0
        small = jnp.zeros((L, L), f32)
        dvs = []
        for h in range(2):
            m = 2 * p + h
            n = index[m]
            fade, enter, cum, cum_row, doc_row, doc_last, cum_last = gates(
                tile, h, columns[:, 4:5], doc_before, columns
            )
            rate = columns[:, 2 + h : 3 + h]
            tail = jnp.where(columns[:, 4:5] == doc_last, jnp.exp(cum_last - cum), 0.0)
            gu = res[m][:L] + fine[m][:L]
            yu = res[m][L : 2 * L] + res[m][2 * L :] + fine[m][L:]
            d_score = d_score + gu[:, :L] * fade
            d_low = d_low - jnp.where(ri > ci, yu[:, :L] * (rate * fade), 0.0)
            dq = dq + enter * gu[:, L:]
            dk = dk + tail * tails[m] - (enter * rate) * yu[:, L:]
            dv = rate * ys[m]
            dvs.append(dv)
            v = active[p * L : (p + 1) * L, (2 + h) * DK : (3 + h) * DK]
            d_cum = jnp.sum(e.o[n] * grads[m].astype(f32) - v * dv, -1, keepdims=True)
            end = jnp.sum(e.st[n + 2] * jnp.transpose(later[m]), -1, keepdims=True)
            end = jnp.sum(end, 0, keepdims=True)
            d_cum = d_cum + jnp.where(ri[:, 0:1] == L - 1, end, 0.0)
            d_rate = jnp.sum(ys[m] * e.u[n], -1, keepdims=True) / rate
            small = small + jnp.where(ci == h, d_cum, 0.0) + jnp.where(ci == 2 + h, d_rate, 0.0)
        scores.append(d_score)
        lows.append(d_low)
        pieces.append([dq, dk, dvs[0], dvs[1], small])
    ks = [split(e.k[pl.ds(x, L), :]) for x in starts]
    qs = [split(e.q[pl.ds(x, L), :]) for x in starts]
    firsts = [
        split(jnp.concatenate([x, y + jnp.transpose(y)], axis=0)) for x, y in zip(scores, lows)
    ]
    firsts = [mm(x, k) for x, k in zip(firsts, ks)]
    seconds = [mm(split(jnp.transpose(x)), q) for x, q in zip(scores, qs)]
    which = lax.broadcasted_iota(jnp.int32, (8, 128), 0)
    for p in range(PER):
        pieces[p][0] = pieces[p][0] + firsts[p][:L]
        pieces[p][1] = pieces[p][1] + firsts[p][L:] + seconds[p]
        small = jnp.transpose(pieces[p].pop())[0:8, :]
        e.daux[PER * i + p] = jnp.where(which < 2, exact(small, lower), small)
    dq, dk, dv0, dv1 = (jnp.concatenate(x, axis=0) for x in zip(*pieces))
    aq, ak = active[:, :DK], active[:, DK : 2 * DK]
    nq = lax.rsqrt(jnp.sum(aq * aq, -1, keepdims=True) + EPS)
    nk = lax.rsqrt(jnp.sum(ak * ak, -1, keepdims=True) + EPS)
    dq = dq * DK**-0.5
    dq = nq * (dq - aq * (nq * nq * jnp.sum(aq * dq, -1, keepdims=True)))
    dk = nk * (dk - ak * (nk * nk * jnp.sum(ak * dk, -1, keepdims=True)))
    d_all = jnp.concatenate([dq, dk, dv0, dv1], axis=1)
    d_sum = d_all * (sigma * (1.0 + sm * (1.0 - sigma)))
    e.gs[8 : 8 + ROWS, :] = d_sum

    x = e.rows[pl.ds(r0, ROWS), :].astype(f32)
    doc = e.cs[8 : 8 + ROWS, 4:5]
    before = e.cs[0:8, 4:5]
    xh = e.halo[i][8:16, :].astype(f32)
    dx = taps[3:4, :] * d_sum
    back = jnp.zeros((8, 4 * DK), f32)
    parts = [jnp.sum(d_sum * x, 0, keepdims=True)]
    for o in (1, 2, 3):
        tap = taps[3 - o : 4 - o, :]
        moved = jnp.where(
            e.cs[8 + o : 8 + o + ROWS, 4:5] == doc, e.gs[8 + o : 8 + o + ROWS, :], 0.0
        )
        dx = dx + tap * moved
        over = jnp.where(e.cs[o : o + 8, 4:5] == before, e.gs[o : o + 8, :], 0.0)
        back = back + tap * over
        parts.append(
            jnp.sum(moved * x, 0, keepdims=True) + jnp.sum(over * xh, 0, keepdims=True)
        )
    rest = jnp.where((t > 0) & (i < CHIPS - 1), e.back[lax.rem(t + 3, CHIPS)], 0.0)
    edge = dx[ROWS - 8 :, :] + rest
    e.dmix[pl.ds(r0, ROWS), :] = jnp.concatenate([dx[: ROWS - 8, :], edge], axis=0).astype(bf16)
    e.edge[t] = edge
    e.back[t] = back
    e.taps[...] = e.taps[...] + jnp.concatenate(parts[::-1], axis=0)


def start_finish(e):
    e.gs[0:8, :] = jnp.zeros((8, 4 * DK), f32)
    e.gs[8 + ROWS :, :] = jnp.zeros((8, 4 * DK), f32)
    e.cs[8 + ROWS :, :] = jnp.full((8, 8), -2.0, f32)
    e.taps[...] = jnp.zeros((4, 4 * DK), f32)
    e.back[...] = jnp.zeros((CHIPS, 8, 4 * DK), f32)


def head_taps(weight, j):
    wq = weight[:, pl.ds(pl.multiple_of(j * DK, DK), DK)]
    wk = weight[:, pl.ds(pl.multiple_of((KH + j) * DK, DK), DK)]
    wv = weight[:, pl.ds(pl.multiple_of((2 * KH + 2 * j) * DK, 2 * DK), 2 * DK)]
    return jnp.concatenate([wq.astype(f32), wk.astype(f32), wv.astype(f32)], axis=1)


SQ = (2 * NB, DK, DK)
SCRATCH = dict(
    rows=((QUARTER, 4 * DK), bf16),
    grad=((QUARTER, 2 * DK), bf16),
    aux=((GROUP, 8, 128), f32),
    halo=((CHIPS, 16, 4 * DK), bf16),
    haux=((CHIPS, 8, 128), f32),
    xs=((8 + ROWS, 4 * DK), f32),
    ds=((8 + ROWS, 8), f32),
    tile=((NB, 8, 128), f32),
    col=((CHIPS, 8 + ROWS, 8), f32),
    summed=((QUARTER, 4 * DK), f32),
    q=((QUARTER, DK), f32),
    k=((QUARTER, DK), f32),
    nh=((2 * NB, 2 * L, L), bf16),
    nl=((2 * NB, 2 * L, L), bf16),
    wh=((2 * NB, 2 * L, DK), bf16),
    wl=((2 * NB, 2 * L, DK), bf16),
    ah=(SQ, bf16),
    al=(SQ, bf16),
    u=(SQ, f32),
    o=(SQ, f32),
    b=(SQ, f32),
    r=(SQ, f32),
    gt=(SQ, bf16),
    st=((2 * NB + 2, DK, DK), f32),
    rt=((2 * NB + 2, DK, DK), f32),
    pi=((2 * NB + 2, DK, DK), f32),
    ps=((2 * NB + 2, DK, DK), f32),
    arrived=((4, DK, DK), f32),
    cs=((16 + ROWS, 8), f32),
    gs=((16 + ROWS, 4 * DK), f32),
    out=((QUARTER, 2 * DK), bf16),
    dmix=((QUARTER, 4 * DK), bf16),
    edge=((CHIPS, 8, 4 * DK), f32),
    back=((CHIPS, 8, 4 * DK), f32),
    taps=((4, 4 * DK), f32),
    daux=((GROUP, 8, 128), f32),
)


ARGS = ("mixed", "weight", "decay", "rate", "docs", "grad_in")
OUTS = ("o_out", "o_mix", "o_taps", "o_decay", "o_rate")
EXTRA = dict(
    aux_own=((GROUP, 8, 128), f32),
    edges=((GROUP, 8, 4 * DK), f32),
    backs=((GROUP, 8, 4 * DK), f32),
    part=((16, 4, 4 * DK), f32),
    total=((4, 4 * DK), f32),
    gathered=((GROUP, 4, 4 * DK), f32),
    daux_in=((GROUP, 8, 128), f32),
)
SEMS = dict(
    asend=(GROUP, 5),
    arecv=(GROUP, 5),
    hsend=(GROUP, 4),
    hrecv=(CHIPS, 4),
    ssend=(2,),
    srecv=(2,),
    bsend=(CHIPS,),
    brecv=(GROUP,),
    esend=(CHIPS,),
    erecv=(GROUP,),
    fsend=(GROUP, 5),
    frecv=(GROUP, 5),
    tsend=(16,),
    trecv=(16,),
    gsend=(GROUP,),
    grecv=(GROUP,),
)
NAMES = ARGS + OUTS + tuple(SCRATCH) + tuple(EXTRA) + tuple(SEMS)


def head_columns(to):
    return (
        pl.ds(pl.multiple_of(to * DK, DK), DK),
        pl.ds(pl.multiple_of((KH + to) * DK, DK), DK),
        pl.ds(pl.multiple_of((2 * KH + 2 * to) * DK, 2 * DK), 2 * DK),
    )


OWN = (pl.ds(0, DK), pl.ds(DK, DK), pl.ds(2 * DK, 2 * DK))


def two_columns(to):
    return pl.ds(pl.multiple_of(to * 2 * DK, 2 * DK), 2 * DK)


def place(j):
    return pl.ds(pl.multiple_of(j * 128, 128), 128)


def layer_kernel(*refs):
    e = types.SimpleNamespace(**dict(zip(NAMES, refs)))
    dp = lax.axis_index("dp")
    me = lax.axis_index("seq")
    row, j = me // GROUP, lax.rem(me, GROUP)
    y, c = j // 2, lax.rem(j, 2)
    base = row * GROUP
    last = GROUP - 1
    before = lax.rem(row + 3, 4) * GROUP
    after = lax.rem(row + 1, 4) * GROUP
    is_last = j == last
    first = (row == 0).astype(jnp.int32)

    def remote(src, dst, send, recv, seq, slab=None):
        return pltpu.make_async_remote_copy(
            src_ref=src,
            dst_ref=dst,
            send_sem=send,
            recv_sem=recv,
            device_id=(dp if slab is None else slab, seq),
            device_id_type=MESH,
        )

    def peer(dy, dc):
        return 2 * lax.rem(y + dy, CHIPS) + lax.rem(c + dc, 2)

    def plane(n):
        return lax.rem(dp + n // 4, 4), lax.rem(me + (n % 4) * GROUP, 4 * GROUP)

    barrier = pltpu.get_barrier_semaphore()

    def greet(slab, seq):
        pl.semaphore_signal(barrier, inc=1, device_id=(slab, seq), device_id_type=MESH)

    for s in range(1, GROUP):
        greet(dp, base + lax.rem(j + s, GROUP))
    for n in range(1, 16):
        greet(*plane(n))
    greet(dp, before + last)

    @pl.when(is_last)
    def _():
        for to in range(GROUP):
            greet(dp, after + to)

    docs = e.docs[...].astype(f32)
    for to in range(GROUP):
        e.aux_own[to] = jnp.concatenate(
            [
                e.decay[2 * to : 2 * to + 2, :],
                e.rate[2 * to : 2 * to + 2, :],
                docs,
                jnp.zeros((3, 128), f32),
            ],
            axis=0,
        )
    taps = head_taps(e.weight, j)
    pl.semaphore_wait(barrier, jnp.where(is_last, GROUP - 1 + 15 + 1 + GROUP, GROUP - 1 + 15 + 1))

    slot = lax.rem(y + 1, CHIPS)
    inside = y < CHIPS - 1
    there = jnp.where(inside, base, after)

    def halo_copies(to, at, group):
        own = head_columns(to)
        r = pl.ds(112, 16)
        pairs = [(e.mixed.at[r, own[n]], e.halo.at[at, :, OWN[n]]) for n in range(3)]
        pairs.append((e.aux_own.at[to], e.haux.at[at]))
        return [
            remote(src, dst, e.hsend.at[to, n], e.hrecv.at[at, n], group + to)
            for n, (src, dst) in enumerate(pairs)
        ]

    @pl.when(c == 1)
    def _():
        for to in range(GROUP):

            @pl.when(jnp.logical_not(inside) | (j != to))
            def _():
                for copy in halo_copies(to, slot, there):
                    copy.start()

        @pl.when(inside)
        def _():
            own = head_columns(j)
            for n in range(3):
                e.halo[slot, :, OWN[n]] = e.mixed[112:128, own[n]]
            e.haux[slot] = e.aux_own[j]

    def dy_of(t):
        return t + t // 2 - 2 * (t // 3)

    def head_copy(t, dc, n):
        to = peer(dy_of(t), dc)
        own = head_columns(to)
        at = place(j)
        src, dst = (
            (e.mixed.at[:, own[0]], e.rows.at[at, OWN[0]]),
            (e.mixed.at[:, own[1]], e.rows.at[at, OWN[1]]),
            (e.mixed.at[:, own[2]], e.rows.at[at, OWN[2]]),
            (e.aux_own.at[to], e.aux.at[j]),
            (e.grad_in.at[:, two_columns(to)], e.grad.at[at, :]),
        )[n]
        k = 2 * t + dc
        return remote(src, dst, e.asend.at[k, n], e.arecv.at[k, n], base + to)

    steps = [(t, dc) for t in range(CHIPS) for dc in range(2) if (t, dc) != (0, 0)]
    for t, dc in steps:
        for n in range(4):
            head_copy(t, dc, n).start()
    for t, dc in steps:
        head_copy(t, dc, 4).start()

    own = head_columns(j)
    for n in range(3):
        e.rows[place(j), OWN[n]] = e.mixed[:, own[n]]
    e.aux[j] = e.aux_own[j]
    e.grad[place(j), :] = e.grad_in[:, two_columns(j)]

    def pair_of(t):
        return lax.rem(y + CHIPS - dy_of(t), CHIPS)

    def prepare(t, carry):
        i = pair_of(t)

        @pl.when(t > 0)
        def _():
            for n in range(4):
                head_copy(t, 0, n).wait_recv()

        for n in range(4):
            head_copy(t, 1, n).wait_recv()

        @pl.when((i == 0) | (2 * i - 1 != j))
        def _():
            for copy in halo_copies(0, i, base):
                copy.wait_recv()

        prepare_pair(e, i, first, taps)
        return carry

    lax.fori_loop(0, CHIPS, prepare, 0)

    def hop(n, src, to):
        return remote(src, e.arrived.at[pl.ds(2 * n, 2)], e.ssend.at[n], e.srecv.at[n], to)

    forth = hop(0, e.st.at[pl.ds(2 * NB, 2)], lax.rem(me + GROUP, 4 * GROUP))
    back = hop(1, e.rt.at[pl.ds(0, 2)], lax.rem(me + 3 * GROUP, 4 * GROUP))
    scan_forward(e)
    start_finish(e)
    forth.start()

    def turn(t, carry):
        @pl.when(t > 0)
        def _():
            head_copy(t, 0, 4).wait_recv()

        head_copy(t, 1, 4).wait_recv()
        backward_terms(e, pair_of(t))
        return carry

    lax.fori_loop(0, CHIPS, turn, 0)
    scan_backward(e)
    for t, dc in steps:
        for n in range(5):
            head_copy(t, dc, n).wait_send()

    @pl.when(c == 1)
    def _():
        for to in range(GROUP):

            @pl.when(jnp.logical_not(inside) | (j != to))
            def _():
                for copy in halo_copies(to, slot, there):
                    copy.wait_send()

    back.start()
    forth.wait()
    last_state(e)

    def token_copy(t, dc, n):
        to = peer(CHIPS - 1 - t, dc)
        r = place(to)
        own = head_columns(j)
        src, dst = (
            (e.out.at[r, :], e.o_out.at[:, two_columns(j)]),
            (e.dmix.at[r, OWN[0]], e.o_mix.at[:, own[0]]),
            (e.dmix.at[r, OWN[1]], e.o_mix.at[:, own[1]]),
            (e.dmix.at[r, OWN[2]], e.o_mix.at[:, own[2]]),
            (e.daux.at[to], e.daux_in.at[j]),
        )[n]
        k = 2 * t + dc
        return remote(src, dst, e.fsend.at[k, n], e.frecv.at[k, n], base + to)

    def target(t):
        return lax.rem(y + CHIPS - 1 - t, CHIPS)

    def read(t, carry):
        read_pair(e, target(t))

        @pl.when(t < CHIPS - 1)
        def _():
            token_copy(t, 0, 0).start()

        token_copy(t, 1, 0).start()
        return carry

    lax.fori_loop(0, CHIPS, read, 0)
    back.wait()

    def edge_copy(i, at):
        return remote(
            e.edge.at[at], e.edges.at[j], e.esend.at[at], e.erecv.at[j], base + 2 * i + 1
        )

    def edge_goes(i, t):
        return ((i == CHIPS - 1) & (j != last)) | ((t == 0) & (i < CHIPS - 1))

    def back_copy(i, at):
        to = jnp.where(i == 0, before + last, base + 2 * i - 1)
        return remote(e.back.at[at], e.backs.at[j], e.bsend.at[at], e.brecv.at[j], to)

    def back_goes(i, t):
        return (i == 0) | (t == CHIPS - 1)

    def finish(t, carry):
        i = target(t)
        finish_pair(e, i, t, taps)

        @pl.when(t < CHIPS - 1)
        def _():
            for n in range(1, 5):
                token_copy(t, 0, n).start()

        for n in range(1, 5):
            token_copy(t, 1, n).start()

        @pl.when(edge_goes(i, t))
        def _():
            edge_copy(i, t).start()

        @pl.when((i == CHIPS - 1) & (j == last))
        def _():
            e.edges[j] = e.edge[t]

        @pl.when(back_goes(i, t))
        def _():
            back_copy(i, t).start()

        return carry

    lax.fori_loop(0, CHIPS, finish, 0)

    spot = 4 * dp + row

    def tap_copy(n):
        slab, seq = plane(n)
        return remote(e.taps.at[:, :], e.part.at[spot], e.tsend.at[n], e.trecv.at[n], seq, slab)

    for n in range(1, 16):
        tap_copy(n).start()

    own = head_columns(j)
    e.o_out[:, two_columns(j)] = e.out[place(j), :]
    for n in range(3):
        e.o_mix[:, own[n]] = e.dmix[place(j), OWN[n]]
    e.daux_in[j] = e.daux[j]

    for n in range(1, 16):
        tap_copy(n).wait_recv()
    e.part[spot] = e.taps[...]
    whole = e.part[0]
    for n in range(1, 16):
        whole = whole + e.part[n]
    e.total[...] = whole
    e.gathered[j] = whole

    def gather_copy(s):
        return remote(
            e.total.at[:, :],
            e.gathered.at[j],
            e.gsend.at[s],
            e.grecv.at[s],
            base + lax.rem(j + s, GROUP),
        )

    for s in range(1, GROUP):
        gather_copy(s).start()

    for t in range(CHIPS):
        for dc in range(2):
            if (t, dc) != (CHIPS - 1, 0):
                for n in range(5):
                    token_copy(t, dc, n).wait()

    @pl.when(c == 1)
    def _():
        for src in range(GROUP):

            def edge_from():
                return remote(
                    e.edge.at[0], e.edges.at[src], e.esend.at[0], e.erecv.at[src], base + last
                )

            def back_from():
                return remote(
                    e.back.at[0], e.backs.at[src], e.bsend.at[0], e.brecv.at[src], base + last
                )

            whole_row = y == CHIPS - 1

            @pl.when(whole_row | (y + 1 == src // 2))
            def _():
                @pl.when(j != src)
                def _():
                    edge_from().wait_recv()

                back_from().wait_recv()
                fixed = e.edges[src] + e.backs[src]
                spots = (
                    (src * DK, DK, 0),
                    ((KH + src) * DK, DK, DK),
                    ((2 * KH + 2 * src) * DK, 2 * DK, 2 * DK),
                )
                for at, width, own_at in spots:
                    old = e.o_mix[112:128, at : at + width].astype(f32)
                    new = jnp.concatenate([old[0:8], fixed[:, own_at : own_at + width]], axis=0)
                    e.o_mix[112:128, at : at + width] = new.astype(bf16)

    for src in range(GROUP):
        e.o_decay[2 * src : 2 * src + 2, :] = e.daux_in[src][0:2, :]
        e.o_rate[2 * src : 2 * src + 2, :] = e.daux_in[src][2:4, :]

    for s in range(1, GROUP):
        gather_copy(s).wait()
    for src in range(GROUP):
        got = e.gathered[src]
        e.o_taps[:, src * DK : (src + 1) * DK] = got[:, 0:DK]
        e.o_taps[:, (KH + src) * DK : (KH + src + 1) * DK] = got[:, DK : 2 * DK]
        e.o_taps[:, (2 * KH + 2 * src) * DK : (2 * KH + 2 * src + 2) * DK] = got[:, 2 * DK :]

    for n in range(1, 16):
        tap_copy(n).wait_send()
    for t in range(CHIPS):
        i = target(t)

        @pl.when(edge_goes(i, t))
        def _():
            edge_copy(i, t).wait_send()

        @pl.when(back_goes(i, t))
        def _():
            back_copy(i, t).wait_send()


def layer(*args):
    scratch = [VM(*x) for x in SCRATCH.values()] + [VM(*x) for x in EXTRA.values()]
    return pl.pallas_call(
        layer_kernel,
        out_shape=(
            jax.ShapeDtypeStruct((128, 2 * KH * DK), bf16),
            jax.ShapeDtypeStruct((128, 4 * KH * DK), bf16),
            jax.ShapeDtypeStruct((4, 4 * KH * DK), f32),
            jax.ShapeDtypeStruct((VH, 128), f32),
            jax.ShapeDtypeStruct((VH, 128), f32),
        ),
        in_specs=[vspec] * len(ARGS),
        out_specs=(vspec,) * len(OUTS),
        scratch_shapes=scratch + [pltpu.SemaphoreType.DMA(x) for x in SEMS.values()],
        compiler_params=pltpu.CompilerParams(
            collective_id=0, has_side_effects=True, vmem_limit_bytes=60 * 1024 * 1024
        ),
        name="layer",
    )(*args)


HALVES = ((0, 0, 128), (1, 0, 64), (1, 64, 64), (2, 0, 4), (3, 0, 16), (4, 0, 16))


def emit_kernel(*refs):
    srcs, dsts, mids, (come, go) = refs[:5], refs[5:10], refs[10:15], refs[15:]
    into, out = [], []
    for n, (a, r, size) in enumerate(HALVES):
        rows = pl.ds(r, size)
        mid = mids[a].at[rows]
        into.append(pltpu.make_async_copy(srcs[a].at[rows], mid, come.at[n]))
        out.append(pltpu.make_async_copy(mid, dsts[a].at[rows], go.at[n]))
    for copy in into:
        copy.start()
    for first, second in zip(into, out):
        first.wait()
        second.start()
    for copy in out:
        copy.wait()


def emit(*arrays):
    far = pl.BlockSpec(memory_space=pl.ANY)
    sems = pltpu.SemaphoreType.DMA((len(HALVES),))
    return pl.pallas_call(
        emit_kernel,
        out_shape=tuple(jax.ShapeDtypeStruct(x.shape, x.dtype) for x in arrays),
        in_specs=[far] * 5,
        out_specs=(far,) * 5,
        scratch_shapes=[VM(x.shape, x.dtype) for x in arrays] + [sems, sems],
        name="emit",
    )(*arrays)


def local(mixed, conv_weight, log_decay, beta, doc_ids, out_grad):
    out, dmix, taps, d_decay, d_beta = layer(
        mixed[0], conv_weight, log_decay[0], beta[0], doc_ids, out_grad[0]
    )
    out, dmix, taps, d_decay, d_beta = emit(out, dmix, taps, d_decay, d_beta)
    return out[None], dmix[None], taps, d_decay[None], d_beta[None]


def solution(mesh):
    in_specs = (
        P("dp", "seq", None),
        P(),
        P("dp", None, "seq"),
        P("dp", None, "seq"),
        P("dp", "seq"),
        P("dp", "seq", None),
    )
    out_specs = (
        P("dp", "seq", None),
        P("dp", "seq", None),
        P(),
        P("dp", None, "seq"),
        P("dp", None, "seq"),
    )
    return jax.shard_map(local, mesh=mesh, in_specs=in_specs, out_specs=out_specs, check_vma=False)
```

```python
import types

import jax
import jax.numpy as jnp
from jax import lax
from jax.experimental import pallas as pl
from jax.experimental.pallas import tpu as pltpu
from jax.sharding import PartitionSpec as P

DK = 128
KH = 8
VH = 16
L = 128
GROUP = 8
CHIPS = GROUP // 2
QUARTER = GROUP * 128
NB = QUARTER // L
PER = 2
ROWS = PER * L
EPS = 1e-6

f32 = jnp.float32
bf16 = jnp.bfloat16
NN = (((1,), (0,)), ((), ()))
NT = (((1,), (1,)), ((), ()))
MESH = pl.DeviceIdType.MESH
VM = pltpu.VMEM
vspec = pl.BlockSpec(memory_space=pltpu.VMEM)


def split(a):
    high = a.astype(bf16)
    return high, (a - high.astype(f32)).astype(bf16)


def stack(*pairs):
    return tuple(jnp.concatenate(x, axis=0) for x in zip(*pairs))


def mm(a, b, dims=NN):
    def dot(p, q):
        return lax.dot_general(p, q, dims, preferred_element_type=f32)

    if len(a) == 1:
        return dot(a[0], b[0]) + dot(a[0], b[1])
    rows = a[0].shape[0]
    both = dot(jnp.concatenate(a, axis=0), b[0])
    return both[:rows] + both[rows:] + dot(a[0], b[1])


def wide(a, b):
    left = jnp.concatenate([a[0], a[1], a[0]], axis=1)
    right = jnp.concatenate([b[0], b[0], b[1]], axis=0)
    return lax.dot_general(left, right, NN, preferred_element_type=f32)


def exact(a, b):
    return lax.dot_general(a, b, NN, preferred_element_type=f32, precision=lax.Precision.HIGHEST)


def iotas(rows=L):
    return (
        lax.broadcasted_iota(jnp.int32, (rows, L), 0),
        lax.broadcasted_iota(jnp.int32, (rows, L), 1),
    )


def invert(lows):
    ri, ci = iotas()
    eye = jnp.where(ri == ci, 1.0, 0.0).astype(f32)
    near = ri // 8 == ci // 8
    d = [jnp.where(near, x, 0.0) for x in lows]
    s1 = [split(x) for x in d]
    d2 = [mm(x, x) for x in s1]
    s2 = [split(x) for x in d2]
    d34 = [mm(stack(x, y), y) for x, y in zip(s1, s2)]
    inverse = [eye - x + y - z[:L] for x, y, z in zip(d, d2, d34)]
    inverse = [x + mm(split(x), split(z[L:])) for x, z in zip(inverse, d34)]
    half, lane = iotas(L // 2)
    size = 8
    while size < L:
        spots = range(0, L, 2 * size)
        mask = lane // size == 2 * (half // size)
        corner = [
            jnp.where(mask, jnp.concatenate([x[r + size : r + 2 * size] for r in spots], 0), 0.0)
            for x in lows
        ]
        inner = [mm(split(c), split(x)) for c, x in zip(corner, inverse)]
        zero = jnp.zeros((size, L), f32)
        spread = [
            jnp.concatenate(
                [p for m in range(len(spots)) for p in (zero, y[m * size : (m + 1) * size])], 0
            )
            for y in inner
        ]
        odd = [jnp.concatenate([x[r + size : r + 2 * size] for r in spots], 0) for x in inverse]
        odd = [x - mm(split(x), split(y)) for x, y in zip(odd, spread)]
        inverse = [
            jnp.concatenate(
                [
                    p
                    for m, r in enumerate(spots)
                    for p in (x[r : r + size], o[m * size : (m + 1) * size])
                ],
                0,
            )
            for x, o in zip(inverse, odd)
        ]
        size *= 2
    return inverse


def gates(tile, h, doc_column, doc_before, columns):
    ri, ci = iotas()
    doc_row = tile[4:5, :]
    cum = columns[:, h : h + 1]
    cum_row = tile[h : h + 1, :]
    doc_last = tile[4:5, L - 1 : L]
    cum_last = tile[h : h + 1, L - 1 : L]
    fade = jnp.where(
        (doc_column == doc_row) & (ri >= ci), jnp.exp(jnp.minimum(cum - cum_row, 0.0)), 0.0
    )
    enter = jnp.where(doc_column == doc_before, jnp.exp(cum), 0.0)
    return fade, enter, cum, cum_row, doc_row, doc_last, cum_last


def prepare_pair(e, i, first, taps):
    ri, ci = iotas()
    r0 = pl.multiple_of(i * ROWS, ROWS)
    e.xs[0:8, :] = e.halo[i][8:16, :].astype(f32)
    e.xs[8:, :] = e.rows[pl.ds(r0, ROWS), :].astype(f32)
    upper = jnp.where(ri <= ci, 1.0, 0.0).astype(f32)
    flat = jnp.concatenate([e.aux[PER * i + p] for p in range(PER)], axis=0)
    sums = exact(flat, upper)
    which = lax.rem(lax.broadcasted_iota(jnp.int32, (PER * 8, 128), 0), 8)
    flat = jnp.where(which < 2, sums, flat)
    tiles = [flat[8 * p : 8 * p + 8] for p in range(PER)]
    edge_columns = jnp.transpose(e.haux[i])[120:128, :]
    at_start = (first + (i == 0).astype(jnp.int32)) == 2
    e.ds[0:8, :] = jnp.where(at_start, -1.0, edge_columns)
    for p in range(PER):
        e.tile[PER * i + p] = tiles[p]
        e.ds[8 + p * L : 8 + (p + 1) * L, :] = jnp.transpose(tiles[p])
    e.col[i] = e.ds[...]
    doc = e.ds[8:, 4:5]
    summed = taps[3:4, :] * e.xs[8:, :]
    for o in (1, 2, 3):
        same = e.ds[8 - o : 8 - o + ROWS, 4:5] == doc
        summed = summed + taps[3 - o : 4 - o, :] * jnp.where(
            same, e.xs[8 - o : 8 - o + ROWS, :], 0.0
        )
    e.summed[pl.ds(r0, ROWS), :] = summed
    active = summed / (1.0 + jnp.exp(-summed))
    q = active[:, :DK]
    k = active[:, DK : 2 * DK]
    q = q * lax.rsqrt(jnp.sum(q * q, -1, keepdims=True) + EPS) * DK**-0.5
    k = k * lax.rsqrt(jnp.sum(k * k, -1, keepdims=True) + EPS)
    e.q[pl.ds(r0, ROWS), :] = q
    e.k[pl.ds(r0, ROWS), :] = k

    chains = []
    for p in range(PER):
        lo = slice(p * L, (p + 1) * L)
        kp, qp = k[lo], q[lo]
        ks = split(kp)
        both = mm(stack(ks, split(qp)), ks, NT)
        inner, score = both[:L], both[L:]
        columns = e.ds[8 + p * L : 8 + (p + 1) * L, :]
        doc_before = e.ds[7 + p * L : 8 + p * L, 4:5]
        turned = jnp.transpose(kp)
        for h in range(2):
            fade, enter, cum, cum_row, doc_row, doc_last, cum_last = gates(
                tiles[p], h, columns[:, 4:5], doc_before, columns
            )
            rate = columns[:, 2 + h : 3 + h]
            tail_row = jnp.where(doc_row == doc_last, jnp.exp(cum_last - cum_row), 0.0)
            keep = jnp.where(doc_last == doc_before, jnp.exp(cum_last), 0.0)
            chains.append(
                dict(
                    n=(PER * i + p) * 2 + h,
                    low=jnp.where(ri > ci, rate * inner * fade, 0.0),
                    left=jnp.concatenate([score * fade, turned * tail_row], axis=0),
                    right=jnp.concatenate(
                        [(rate * enter) * kp, rate * active[lo, (2 + h) * DK : (3 + h) * DK]], axis=1
                    ),
                    eq=enter * qp,
                    keep=keep,
                )
            )
    inverse = [split(t) for t in invert([c["low"] for c in chains])]
    lefts = [split(mm(split(c["left"]), t)) for c, t in zip(chains, inverse)]
    bigs = [wide(stack(t, x), split(c["right"])) for c, t, x in zip(chains, inverse, lefts)]
    for c, ns, big in zip(chains, lefts, bigs):
        n = c["n"]
        e.nh[n] = ns[0]
        e.nl[n] = ns[1]
        ws = split(jnp.concatenate([big[:L, :DK], c["eq"] - big[L : 2 * L, :DK]], axis=0))
        e.wh[n] = ws[0]
        e.wl[n] = ws[1]
        e.u[n] = big[:L, DK:]
        e.o[n] = big[L : 2 * L, DK:]
        a = split(jnp.where(ri == ci, c["keep"], 0.0) - big[2 * L :, :DK])
        e.ah[n] = a[0]
        e.al[n] = a[1]
        e.b[n] = big[2 * L :, DK:]


def backward_terms(e, i):
    spots = [(p, h) for p in range(PER) for h in range(2)]
    index = [2 * (PER * i + p) + h for p, h in spots]
    starts = [pl.multiple_of(i * ROWS + p * L, L) for p in range(PER)]
    grads = [e.grad[pl.ds(starts[p], L), h * DK : (h + 1) * DK] for p, h in spots]
    turned = [jnp.transpose(g.astype(f32)).astype(bf16) for g in grads]
    terms = [mm((g,), (e.wh[n][L:], e.wl[n][L:])) for n, g in zip(index, turned)]
    for n, g, r in zip(index, turned, terms):
        e.gt[n] = g
        e.r[n] = r


def scan_forward(e):
    ri, ci = iotas()
    eye = jnp.where(ri == ci, 1.0, 0.0).astype(f32)
    for h in range(2):
        e.st[h] = jnp.zeros((DK, DK), f32)
        e.pi[h] = eye

    def step(i, carry):
        for h in range(2):
            n = 2 * i + h
            got = wide((e.ah[n], e.al[n]), split(jnp.concatenate([e.st[n], e.pi[n]], axis=1)))
            e.st[n + 2] = got[:, :DK] + e.b[n]
            e.pi[n + 2] = got[:, DK:]
        return carry

    lax.fori_loop(0, NB, step, 0)


def scan_backward(e):
    ri, ci = iotas()
    eye = jnp.where(ri == ci, 1.0, 0.0).astype(f32)
    for h in range(2):
        e.rt[2 * NB + h] = jnp.zeros((DK, DK), f32)
        e.ps[2 * NB + h] = eye

    def step(i, carry):
        for h in range(2):
            n = 2 * (NB - 1 - i) + h
            got = mm(split(jnp.concatenate([e.rt[n + 2], e.ps[n + 2]], axis=0)), (e.ah[n], e.al[n]))
            e.rt[n] = got[:DK] + e.r[n]
            e.ps[n] = got[DK:]
        return carry

    lax.fori_loop(0, NB, step, 0)


def last_state(e):
    for h in range(2):
        e.st[2 * NB + h] = e.st[2 * NB + h] + mm(split(e.pi[2 * NB + h]), split(e.arrived[h]))


def read_pair(e, i):
    entered = [split(e.arrived[h]) for h in range(2)]
    spots = [(p, h) for p in range(PER) for h in range(2)]
    index = [2 * (PER * i + p) + h for p, h in spots]
    states = [
        e.st[n] + mm(split(e.pi[n]), entered[h]) for n, (p, h) in zip(index, spots)
    ]
    both = [mm((e.wh[n], e.wl[n]), split(x)) for n, x in zip(index, states)]
    for n, (p, h), state, x in zip(index, spots, states, both):
        rb = pl.multiple_of(i * ROWS + p * L, L)
        e.st[n] = state
        e.u[n] = e.u[n] - x[:L]
        out = e.o[n] + x[L:]
        e.o[n] = out
        e.out[pl.ds(rb, L), h * DK : (h + 1) * DK] = out.astype(bf16)


def finish_pair(e, i, t, taps):
    ri, ci = iotas()
    lower = jnp.where(ri >= ci, 1.0, 0.0).astype(f32)
    r0 = pl.multiple_of(i * ROWS, ROWS)
    e.cs[0 : 8 + ROWS, :] = e.col[i]
    sm = e.summed[pl.ds(r0, ROWS), :]
    sigma = 1.0 / (1.0 + jnp.exp(-sm))
    active = sm * sigma
    left = [split(e.arrived[2 + h]) for h in range(2)]

    def dot(a, b):
        return lax.dot_general(a, b, NT, preferred_element_type=f32)

    spots = [(p, h) for p in range(PER) for h in range(2)]
    index = [2 * (PER * i + p) + h for p, h in spots]
    starts = [pl.multiple_of(r0 + p * L, L) for p in range(PER)]
    later = [
        e.rt[n + 2] + mm(left[h], split(e.ps[n + 2])) for (p, h), n in zip(spots, index)
    ]
    laters = [split(x) for x in later]
    turned = [
        mm((e.gt[n],), (e.nh[n][:L], e.nl[n][:L])) + mm(x, (e.nh[n][L:], e.nl[n][L:]))
        for n, x in zip(index, laters)
    ]
    ys = [jnp.transpose(x) for x in turned]
    us = [split(e.u[n]) for n in index]
    states = [split(e.st[n]) for n in index]
    grads = [e.grad[pl.ds(starts[p], L), h * DK : (h + 1) * DK] for p, h in spots]
    tops = [jnp.concatenate((g,) + split(y), axis=0) for g, y in zip(grads, ys)]
    rights = [stack(u, x) for u, x in zip(us, states)]
    res = [dot(a, b[0]) for a, b in zip(tops, rights)]
    fine = [dot(a[: 2 * L], b[1]) for a, b in zip(tops, rights)]
    tails = [mm(u, x) for u, x in zip(us, laters)]
    pieces, scores, lows = [], [], []
    for p in range(PER):
        block = PER * i + p
        rb = starts[p]
        tile = e.tile[block]
        columns = e.cs[8 + p * L : 8 + (p + 1) * L, :]
        doc_before = e.cs[7 + p * L : 8 + p * L, 4:5]
        d_score = d_low = dq = dk = 0.0
        small = jnp.zeros((L, L), f32)
        dvs = []
        for h in range(2):
            m = 2 * p + h
            n = index[m]
            fade, enter, cum, cum_row, doc_row, doc_last, cum_last = gates(
                tile, h, columns[:, 4:5], doc_before, columns
            )
            rate = columns[:, 2 + h : 3 + h]
            tail = jnp.where(columns[:, 4:5] == doc_last, jnp.exp(cum_last - cum), 0.0)
            gu = res[m][:L] + fine[m][:L]
            yu = res[m][L : 2 * L] + res[m][2 * L :] + fine[m][L:]
            d_score = d_score + gu[:, :L] * fade
            d_low = d_low - jnp.where(ri > ci, yu[:, :L] * (rate * fade), 0.0)
            dq = dq + enter * gu[:, L:]
            dk = dk + tail * tails[m] - (enter * rate) * yu[:, L:]
            dv = rate * ys[m]
            dvs.append(dv)
            v = active[p * L : (p + 1) * L, (2 + h) * DK : (3 + h) * DK]
            d_cum = jnp.sum(e.o[n] * grads[m].astype(f32) - v * dv, -1, keepdims=True)
            end = jnp.sum(e.st[n + 2] * jnp.transpose(later[m]), -1, keepdims=True)
            end = jnp.sum(end, 0, keepdims=True)
            d_cum = d_cum + jnp.where(ri[:, 0:1] == L - 1, end, 0.0)
            d_rate = jnp.sum(ys[m] * e.u[n], -1, keepdims=True) / rate
            small = small + jnp.where(ci == h, d_cum, 0.0) + jnp.where(ci == 2 + h, d_rate, 0.0)
        scores.append(d_score)
        lows.append(d_low)
        pieces.append([dq, dk, dvs[0], dvs[1], small])
    ks = [split(e.k[pl.ds(x, L), :]) for x in starts]
    qs = [split(e.q[pl.ds(x, L), :]) for x in starts]
    firsts = [
        split(jnp.concatenate([x, y + jnp.transpose(y)], axis=0)) for x, y in zip(scores, lows)
    ]
    firsts = [mm(x, k) for x, k in zip(firsts, ks)]
    seconds = [mm(split(jnp.transpose(x)), q) for x, q in zip(scores, qs)]
    which = lax.broadcasted_iota(jnp.int32, (8, 128), 0)
    for p in range(PER):
        pieces[p][0] = pieces[p][0] + firsts[p][:L]
        pieces[p][1] = pieces[p][1] + firsts[p][L:] + seconds[p]
        small = jnp.transpose(pieces[p].pop())[0:8, :]
        e.daux[PER * i + p] = jnp.where(which < 2, exact(small, lower), small)
    dq, dk, dv0, dv1 = (jnp.concatenate(x, axis=0) for x in zip(*pieces))
    aq, ak = active[:, :DK], active[:, DK : 2 * DK]
    nq = lax.rsqrt(jnp.sum(aq * aq, -1, keepdims=True) + EPS)
    nk = lax.rsqrt(jnp.sum(ak * ak, -1, keepdims=True) + EPS)
    dq = dq * DK**-0.5
    dq = nq * (dq - aq * (nq * nq * jnp.sum(aq * dq, -1, keepdims=True)))
    dk = nk * (dk - ak * (nk * nk * jnp.sum(ak * dk, -1, keepdims=True)))
    d_all = jnp.concatenate([dq, dk, dv0, dv1], axis=1)
    d_sum = d_all * (sigma * (1.0 + sm * (1.0 - sigma)))
    e.gs[8 : 8 + ROWS, :] = d_sum

    x = e.rows[pl.ds(r0, ROWS), :].astype(f32)
    doc = e.cs[8 : 8 + ROWS, 4:5]
    before = e.cs[0:8, 4:5]
    xh = e.halo[i][8:16, :].astype(f32)
    dx = taps[3:4, :] * d_sum
    back = jnp.zeros((8, 4 * DK), f32)
    parts = [jnp.sum(d_sum * x, 0, keepdims=True)]
    for o in (1, 2, 3):
        tap = taps[3 - o : 4 - o, :]
        moved = jnp.where(
            e.cs[8 + o : 8 + o + ROWS, 4:5] == doc, e.gs[8 + o : 8 + o + ROWS, :], 0.0
        )
        dx = dx + tap * moved
        over = jnp.where(e.cs[o : o + 8, 4:5] == before, e.gs[o : o + 8, :], 0.0)
        back = back + tap * over
        parts.append(
            jnp.sum(moved * x, 0, keepdims=True) + jnp.sum(over * xh, 0, keepdims=True)
        )
    rest = jnp.where((t > 0) & (i < CHIPS - 1), e.back[lax.rem(t + 3, CHIPS)], 0.0)
    edge = dx[ROWS - 8 :, :] + rest
    e.dmix[pl.ds(r0, ROWS), :] = jnp.concatenate([dx[: ROWS - 8, :], edge], axis=0).astype(bf16)
    e.edge[t] = edge
    e.back[t] = back
    e.taps[...] = e.taps[...] + jnp.concatenate(parts[::-1], axis=0)


def start_finish(e):
    e.gs[0:8, :] = jnp.zeros((8, 4 * DK), f32)
    e.gs[8 + ROWS :, :] = jnp.zeros((8, 4 * DK), f32)
    e.cs[8 + ROWS :, :] = jnp.full((8, 8), -2.0, f32)
    e.taps[...] = jnp.zeros((4, 4 * DK), f32)
    e.back[...] = jnp.zeros((CHIPS, 8, 4 * DK), f32)


def head_taps(weight, j):
    wq = weight[:, pl.ds(pl.multiple_of(j * DK, DK), DK)]
    wk = weight[:, pl.ds(pl.multiple_of((KH + j) * DK, DK), DK)]
    wv = weight[:, pl.ds(pl.multiple_of((2 * KH + 2 * j) * DK, 2 * DK), 2 * DK)]
    return jnp.concatenate([wq.astype(f32), wk.astype(f32), wv.astype(f32)], axis=1)


SQ = (2 * NB, DK, DK)
SCRATCH = dict(
    rows=((QUARTER, 4 * DK), bf16),
    grad=((QUARTER, 2 * DK), bf16),
    aux=((GROUP, 8, 128), f32),
    halo=((CHIPS, 16, 4 * DK), bf16),
    haux=((CHIPS, 8, 128), f32),
    xs=((8 + ROWS, 4 * DK), f32),
    ds=((8 + ROWS, 8), f32),
    tile=((NB, 8, 128), f32),
    col=((CHIPS, 8 + ROWS, 8), f32),
    summed=((QUARTER, 4 * DK), f32),
    q=((QUARTER, DK), f32),
    k=((QUARTER, DK), f32),
    nh=((2 * NB, 2 * L, L), bf16),
    nl=((2 * NB, 2 * L, L), bf16),
    wh=((2 * NB, 2 * L, DK), bf16),
    wl=((2 * NB, 2 * L, DK), bf16),
    ah=(SQ, bf16),
    al=(SQ, bf16),
    u=(SQ, f32),
    o=(SQ, f32),
    b=(SQ, f32),
    r=(SQ, f32),
    gt=(SQ, bf16),
    st=((2 * NB + 2, DK, DK), f32),
    rt=((2 * NB + 2, DK, DK), f32),
    pi=((2 * NB + 2, DK, DK), f32),
    ps=((2 * NB + 2, DK, DK), f32),
    arrived=((4, DK, DK), f32),
    cs=((16 + ROWS, 8), f32),
    gs=((16 + ROWS, 4 * DK), f32),
    out=((QUARTER, 2 * DK), bf16),
    dmix=((QUARTER, 4 * DK), bf16),
    edge=((CHIPS, 8, 4 * DK), f32),
    back=((CHIPS, 8, 4 * DK), f32),
    taps=((4, 4 * DK), f32),
    daux=((GROUP, 8, 128), f32),
)


ARGS = ("mixed", "weight", "decay", "rate", "docs", "grad_in")
OUTS = ("o_out", "o_mix", "o_taps", "o_decay", "o_rate")
EXTRA = dict(
    aux_own=((GROUP, 8, 128), f32),
    edges=((GROUP, 8, 4 * DK), f32),
    backs=((GROUP, 8, 4 * DK), f32),
    part=((16, 4, 4 * DK), f32),
    total=((4, 4 * DK), f32),
    gathered=((GROUP, 4, 4 * DK), f32),
    daux_in=((GROUP, 8, 128), f32),
)
SEMS = dict(
    asend=(GROUP, 5),
    arecv=(GROUP, 5),
    hsend=(GROUP, 4),
    hrecv=(CHIPS, 4),
    ssend=(2,),
    srecv=(2,),
    bsend=(CHIPS,),
    brecv=(GROUP,),
    esend=(CHIPS,),
    erecv=(GROUP,),
    fsend=(GROUP, 5),
    frecv=(GROUP, 5),
    tsend=(16,),
    trecv=(16,),
    gsend=(GROUP,),
    grecv=(GROUP,),
)
NAMES = ARGS + OUTS + tuple(SCRATCH) + tuple(EXTRA) + tuple(SEMS)


def head_columns(to):
    return (
        pl.ds(pl.multiple_of(to * DK, DK), DK),
        pl.ds(pl.multiple_of((KH + to) * DK, DK), DK),
        pl.ds(pl.multiple_of((2 * KH + 2 * to) * DK, 2 * DK), 2 * DK),
    )


OWN = (pl.ds(0, DK), pl.ds(DK, DK), pl.ds(2 * DK, 2 * DK))


def two_columns(to):
    return pl.ds(pl.multiple_of(to * 2 * DK, 2 * DK), 2 * DK)


def place(j):
    return pl.ds(pl.multiple_of(j * 128, 128), 128)


def layer_kernel(*refs):
    e = types.SimpleNamespace(**dict(zip(NAMES, refs)))
    dp = lax.axis_index("dp")
    me = lax.axis_index("seq")
    row, j = me // GROUP, lax.rem(me, GROUP)
    y, c = j // 2, lax.rem(j, 2)
    base = row * GROUP
    last = GROUP - 1
    before = lax.rem(row + 3, 4) * GROUP
    after = lax.rem(row + 1, 4) * GROUP
    is_last = j == last
    first = (row == 0).astype(jnp.int32)

    def remote(src, dst, send, recv, seq, slab=None):
        return pltpu.make_async_remote_copy(
            src_ref=src,
            dst_ref=dst,
            send_sem=send,
            recv_sem=recv,
            device_id=(dp if slab is None else slab, seq),
            device_id_type=MESH,
        )

    def peer(dy, dc):
        return 2 * lax.rem(y + dy, CHIPS) + lax.rem(c + dc, 2)

    def plane(n):
        return lax.rem(dp + n // 4, 4), lax.rem(me + (n % 4) * GROUP, 4 * GROUP)

    barrier = pltpu.get_barrier_semaphore()

    def greet(slab, seq):
        pl.semaphore_signal(barrier, inc=1, device_id=(slab, seq), device_id_type=MESH)

    for s in range(1, GROUP):
        greet(dp, base + lax.rem(j + s, GROUP))
    for n in range(1, 16):
        greet(*plane(n))
    greet(dp, before + last)

    @pl.when(is_last)
    def _():
        for to in range(GROUP):
            greet(dp, after + to)

    docs = e.docs[...].astype(f32)
    for to in range(GROUP):
        e.aux_own[to] = jnp.concatenate(
            [
                e.decay[2 * to : 2 * to + 2, :],
                e.rate[2 * to : 2 * to + 2, :],
                docs,
                jnp.zeros((3, 128), f32),
            ],
            axis=0,
        )
    taps = head_taps(e.weight, j)
    pl.semaphore_wait(barrier, jnp.where(is_last, GROUP - 1 + 15 + 1 + GROUP, GROUP - 1 + 15 + 1))

    slot = lax.rem(y + 1, CHIPS)
    inside = y < CHIPS - 1
    there = jnp.where(inside, base, after)

    def halo_copies(to, at, group):
        own = head_columns(to)
        r = pl.ds(112, 16)
        pairs = [(e.mixed.at[r, own[n]], e.halo.at[at, :, OWN[n]]) for n in range(3)]
        pairs.append((e.aux_own.at[to], e.haux.at[at]))
        return [
            remote(src, dst, e.hsend.at[to, n], e.hrecv.at[at, n], group + to)
            for n, (src, dst) in enumerate(pairs)
        ]

    @pl.when(c == 1)
    def _():
        for to in range(GROUP):

            @pl.when(jnp.logical_not(inside) | (j != to))
            def _():
                for copy in halo_copies(to, slot, there):
                    copy.start()

        @pl.when(inside)
        def _():
            own = head_columns(j)
            for n in range(3):
                e.halo[slot, :, OWN[n]] = e.mixed[112:128, own[n]]
            e.haux[slot] = e.aux_own[j]

    def dy_of(t):
        return t + t // 2 - 2 * (t // 3)

    def head_copy(t, dc, n):
        to = peer(dy_of(t), dc)
        own = head_columns(to)
        at = place(j)
        src, dst = (
            (e.mixed.at[:, own[0]], e.rows.at[at, OWN[0]]),
            (e.mixed.at[:, own[1]], e.rows.at[at, OWN[1]]),
            (e.mixed.at[:, own[2]], e.rows.at[at, OWN[2]]),
            (e.aux_own.at[to], e.aux.at[j]),
            (e.grad_in.at[:, two_columns(to)], e.grad.at[at, :]),
        )[n]
        k = 2 * t + dc
        return remote(src, dst, e.asend.at[k, n], e.arecv.at[k, n], base + to)

    steps = [(t, dc) for t in range(CHIPS) for dc in range(2) if (t, dc) != (0, 0)]
    for t, dc in steps:
        for n in range(4):
            head_copy(t, dc, n).start()
    for t, dc in steps:
        head_copy(t, dc, 4).start()

    own = head_columns(j)
    for n in range(3):
        e.rows[place(j), OWN[n]] = e.mixed[:, own[n]]
    e.aux[j] = e.aux_own[j]
    e.grad[place(j), :] = e.grad_in[:, two_columns(j)]

    def pair_of(t):
        return lax.rem(y + CHIPS - dy_of(t), CHIPS)

    def prepare(t, carry):
        i = pair_of(t)

        @pl.when(t > 0)
        def _():
            for n in range(4):
                head_copy(t, 0, n).wait_recv()

        for n in range(4):
            head_copy(t, 1, n).wait_recv()

        @pl.when((i == 0) | (2 * i - 1 != j))
        def _():
            for copy in halo_copies(0, i, base):
                copy.wait_recv()

        prepare_pair(e, i, first, taps)
        return carry

    lax.fori_loop(0, CHIPS, prepare, 0)

    def hop(n, src, to):
        return remote(src, e.arrived.at[pl.ds(2 * n, 2)], e.ssend.at[n], e.srecv.at[n], to)

    forth = hop(0, e.st.at[pl.ds(2 * NB, 2)], lax.rem(me + GROUP, 4 * GROUP))
    back = hop(1, e.rt.at[pl.ds(0, 2)], lax.rem(me + 3 * GROUP, 4 * GROUP))
    scan_forward(e)
    start_finish(e)
    forth.start()

    def turn(t, carry):
        @pl.when(t > 0)
        def _():
            head_copy(t, 0, 4).wait_recv()

        head_copy(t, 1, 4).wait_recv()
        backward_terms(e, pair_of(t))
        return carry

    lax.fori_loop(0, CHIPS, turn, 0)
    scan_backward(e)
    for t, dc in steps:
        for n in range(5):
            head_copy(t, dc, n).wait_send()

    @pl.when(c == 1)
    def _():
        for to in range(GROUP):

            @pl.when(jnp.logical_not(inside) | (j != to))
            def _():
                for copy in halo_copies(to, slot, there):
                    copy.wait_send()

    back.start()
    forth.wait()
    last_state(e)

    def token_copy(t, dc, n):
        to = peer(CHIPS - 1 - t, dc)
        r = place(to)
        own = head_columns(j)
        src, dst = (
            (e.out.at[r, :], e.o_out.at[:, two_columns(j)]),
            (e.dmix.at[r, OWN[0]], e.o_mix.at[:, own[0]]),
            (e.dmix.at[r, OWN[1]], e.o_mix.at[:, own[1]]),
            (e.dmix.at[r, OWN[2]], e.o_mix.at[:, own[2]]),
            (e.daux.at[to], e.daux_in.at[j]),
        )[n]
        k = 2 * t + dc
        return remote(src, dst, e.fsend.at[k, n], e.frecv.at[k, n], base + to)

    def target(t):
        return lax.rem(y + CHIPS - 1 - t, CHIPS)

    def read(t, carry):
        read_pair(e, target(t))

        @pl.when(t < CHIPS - 1)
        def _():
            token_copy(t, 0, 0).start()

        token_copy(t, 1, 0).start()
        return carry

    lax.fori_loop(0, CHIPS, read, 0)
    back.wait()

    def edge_copy(i, at):
        return remote(
            e.edge.at[at], e.edges.at[j], e.esend.at[at], e.erecv.at[j], base + 2 * i + 1
        )

    def edge_goes(i, t):
        return ((i == CHIPS - 1) & (j != last)) | ((t == 0) & (i < CHIPS - 1))

    def back_copy(i, at):
        to = jnp.where(i == 0, before + last, base + 2 * i - 1)
        return remote(e.back.at[at], e.backs.at[j], e.bsend.at[at], e.brecv.at[j], to)

    def back_goes(i, t):
        return (i == 0) | (t == CHIPS - 1)

    def finish(t, carry):
        i = target(t)
        finish_pair(e, i, t, taps)

        @pl.when(t < CHIPS - 1)
        def _():
            for n in range(1, 5):
                token_copy(t, 0, n).start()

        for n in range(1, 5):
            token_copy(t, 1, n).start()

        @pl.when(edge_goes(i, t))
        def _():
            edge_copy(i, t).start()

        @pl.when((i == CHIPS - 1) & (j == last))
        def _():
            e.edges[j] = e.edge[t]

        @pl.when(back_goes(i, t))
        def _():
            back_copy(i, t).start()

        return carry

    lax.fori_loop(0, CHIPS, finish, 0)

    spot = 4 * dp + row

    def tap_copy(n):
        slab, seq = plane(n)
        return remote(e.taps.at[:, :], e.part.at[spot], e.tsend.at[n], e.trecv.at[n], seq, slab)

    for n in range(1, 16):
        tap_copy(n).start()

    own = head_columns(j)
    e.o_out[:, two_columns(j)] = e.out[place(j), :]
    for n in range(3):
        e.o_mix[:, own[n]] = e.dmix[place(j), OWN[n]]
    e.daux_in[j] = e.daux[j]

    for n in range(1, 16):
        tap_copy(n).wait_recv()
    e.part[spot] = e.taps[...]
    whole = e.part[0]
    for n in range(1, 16):
        whole = whole + e.part[n]
    e.total[...] = whole
    e.gathered[j] = whole

    def gather_copy(s):
        return remote(
            e.total.at[:, :],
            e.gathered.at[j],
            e.gsend.at[s],
            e.grecv.at[s],
            base + lax.rem(j + s, GROUP),
        )

    for s in range(1, GROUP):
        gather_copy(s).start()

    for t in range(CHIPS):
        for dc in range(2):
            if (t, dc) != (CHIPS - 1, 0):
                for n in range(5):
                    token_copy(t, dc, n).wait()

    @pl.when(c == 1)
    def _():
        for src in range(GROUP):

            def edge_from():
                return remote(
                    e.edge.at[0], e.edges.at[src], e.esend.at[0], e.erecv.at[src], base + last
                )

            def back_from():
                return remote(
                    e.back.at[0], e.backs.at[src], e.bsend.at[0], e.brecv.at[src], base + last
                )

            whole_row = y == CHIPS - 1

            @pl.when(whole_row | (y + 1 == src // 2))
            def _():
                @pl.when(j != src)
                def _():
                    edge_from().wait_recv()

                back_from().wait_recv()
                fixed = e.edges[src] + e.backs[src]
                spots = (
                    (src * DK, DK, 0),
                    ((KH + src) * DK, DK, DK),
                    ((2 * KH + 2 * src) * DK, 2 * DK, 2 * DK),
                )
                for at, width, own_at in spots:
                    old = e.o_mix[112:128, at : at + width].astype(f32)
                    new = jnp.concatenate([old[0:8], fixed[:, own_at : own_at + width]], axis=0)
                    e.o_mix[112:128, at : at + width] = new.astype(bf16)

    for src in range(GROUP):
        e.o_decay[2 * src : 2 * src + 2, :] = e.daux_in[src][0:2, :]
        e.o_rate[2 * src : 2 * src + 2, :] = e.daux_in[src][2:4, :]

    for s in range(1, GROUP):
        gather_copy(s).wait()
    for src in range(GROUP):
        got = e.gathered[src]
        e.o_taps[:, src * DK : (src + 1) * DK] = got[:, 0:DK]
        e.o_taps[:, (KH + src) * DK : (KH + src + 1) * DK] = got[:, DK : 2 * DK]
        e.o_taps[:, (2 * KH + 2 * src) * DK : (2 * KH + 2 * src + 2) * DK] = got[:, 2 * DK :]

    for n in range(1, 16):
        tap_copy(n).wait_send()
    for t in range(CHIPS):
        i = target(t)

        @pl.when(edge_goes(i, t))
        def _():
            edge_copy(i, t).wait_send()

        @pl.when(back_goes(i, t))
        def _():
            back_copy(i, t).wait_send()


def layer(*args):
    scratch = [VM(*x) for x in SCRATCH.values()] + [VM(*x) for x in EXTRA.values()]
    return pl.pallas_call(
        layer_kernel,
        out_shape=(
            jax.ShapeDtypeStruct((128, 2 * KH * DK), bf16),
            jax.ShapeDtypeStruct((128, 4 * KH * DK), bf16),
            jax.ShapeDtypeStruct((4, 4 * KH * DK), f32),
            jax.ShapeDtypeStruct((VH, 128), f32),
            jax.ShapeDtypeStruct((VH, 128), f32),
        ),
        in_specs=[vspec] * len(ARGS),
        out_specs=(vspec,) * len(OUTS),
        scratch_shapes=scratch + [pltpu.SemaphoreType.DMA(x) for x in SEMS.values()],
        compiler_params=pltpu.CompilerParams(
            collective_id=0, has_side_effects=True, vmem_limit_bytes=60 * 1024 * 1024
        ),
        name="layer",
    )(*args)


HALVES = ((0, 0, 128), (1, 0, 64), (1, 64, 64), (2, 0, 4), (3, 0, 16), (4, 0, 16))


def emit_kernel(*refs):
    srcs, dsts, mids, (come, go) = refs[:5], refs[5:10], refs[10:15], refs[15:]
    into, out = [], []
    for n, (a, r, size) in enumerate(HALVES):
        rows = pl.ds(r, size)
        mid = mids[a].at[rows]
        into.append(pltpu.make_async_copy(srcs[a].at[rows], mid, come.at[n]))
        out.append(pltpu.make_async_copy(mid, dsts[a].at[rows], go.at[n]))
    for copy in into:
        copy.start()
    for first, second in zip(into, out):
        first.wait()
        second.start()
    for copy in out:
        copy.wait()


def emit(*arrays):
    far = pl.BlockSpec(memory_space=pl.ANY)
    sems = pltpu.SemaphoreType.DMA((len(HALVES),))
    return pl.pallas_call(
        emit_kernel,
        out_shape=tuple(jax.ShapeDtypeStruct(x.shape, x.dtype) for x in arrays),
        in_specs=[far] * 5,
        out_specs=(far,) * 5,
        scratch_shapes=[VM(x.shape, x.dtype) for x in arrays] + [sems, sems],
        name="emit",
    )(*arrays)


def local(mixed, conv_weight, log_decay, beta, doc_ids, out_grad):
    out, dmix, taps, d_decay, d_beta = layer(
        mixed[0], conv_weight, log_decay[0], beta[0], doc_ids, out_grad[0]
    )
    out, dmix, taps, d_decay, d_beta = emit(out, dmix, taps, d_decay, d_beta)
    return out[None], dmix[None], taps, d_decay[None], d_beta[None]


def solution(mesh):
    in_specs = (
        P("dp", "seq", None),
        P(),
        P("dp", None, "seq"),
        P("dp", None, "seq"),
        P("dp", "seq"),
        P("dp", "seq", None),
    )
    out_specs = (
        P("dp", "seq", None),
        P("dp", "seq", None),
        P(),
        P("dp", None, "seq"),
        P("dp", None, "seq"),
    )
    return jax.shard_map(local, mesh=mesh, in_specs=in_specs, out_specs=out_specs, check_vma=False)
```
